32 devices in a mesh: seq: 8 (over z, core), head: 4 (over y, x).
Axes of the slice: x: 2, y: 2, z: 4, core: 2. Of those that a mesh axis runs over, the one named last changes fastest.
Arguments:
- mixer_input: bfloat16 [2048, 4096], P('seq', 'head'), may hold values from -600 to 600
- gate_input: bfloat16 [2048, 4096], P('seq', 'head'), may hold values from -5 to 5
- b_proj: bfloat16 [2048, 128], P('seq'), may hold values from -0.5 to 0.5
- c_proj: bfloat16 [2048, 128], P('seq'), may hold values from -0.5 to 0.5
- decay_codes: int32 [64, 2048], P('head', 'seq'), may hold values from 1 to 4096
- decay_rates: float32 [64], P('head'), may hold values from 0 to 1
- skip_gain: float32 [64], P('head'), may hold values from 0.5 to 1.5
- norm_gain: float32 [4096], P('head'), may hold values from 0.5 to 1.5
- queries: bfloat16 [2048, 4096], P('seq', 'head'), may hold values from -5 to 5
- keys: bfloat16 [2048, 4096], P('seq', 'head'), may hold values from -5 to 5
Outputs:
- mamba_out: bfloat16 [2048, 4096], P('seq', 'head')
- attn_out: bfloat16 [2048, 4096], P('seq', 'head')
The draws below stay inside these ranges and needn't reach their ends.
All inputs are finite; a program needn't handle non-finite values.
Results may differ from the reference program's by a relative error of at most 0.013.
Values may be sent and summed in bfloat16 or wider, within the bound.
No kernel may reach another device: no remote copies, remote signals or barrier semaphores. Data moves between devices by JAX's collectives and lax.ppermute only.
A program may use at most 64 MiB of HBM per device.

```python
import math
import jax
import jax.numpy as jnp
from jax import lax

HEADS = 32
HD = 128
CHANNELS_PER_HD = 64
D_STATE = 128
BLOCK = 256
D_INNER = 4096
SSM_HEADS = 64
ITEM_COUNT = 2048


def draw_mixer_input(key, part):
    noise_key = jax.random.fold_in(key, 101)
    row_key = jax.random.fold_in(key, 102)
    columns = jnp.arange(D_INNER, dtype=jnp.float32) / (D_INNER - 1)
    noise = jnp.clip(jax.random.normal(noise_key, (ITEM_COUNT, D_INNER), jnp.float32), -4.0, 4.0)
    column_scale = 10.0 ** columns
    row_scale = 10.0 ** jax.random.uniform(row_key, (ITEM_COUNT, 1), jnp.float32)
    return (noise * column_scale[None, :] * row_scale).astype(jnp.bfloat16)


def draw_decay_rates(key, part):
    pick_key = jax.random.fold_in(key, 301)
    fast_key = jax.random.fold_in(key, 302)
    slow_key = jax.random.fold_in(key, 303)
    fast_share = 0.5
    is_fast = jax.random.uniform(pick_key, (SSM_HEADS,), jnp.float32) < fast_share
    fast_rate = 0.008 * 2.5 ** jax.random.uniform(fast_key, (SSM_HEADS,), jnp.float32)
    slow_rate = 0.1 * 3.5 ** jax.random.uniform(slow_key, (SSM_HEADS,), jnp.float32) / ITEM_COUNT
    return jnp.where(is_fast, fast_rate, slow_rate).astype(jnp.float32)


def draw_decay_codes(key, part):
    base_key = jax.random.fold_in(key, 401)
    layout_seed = jax.random.fold_in(key, 402)
    target_classes = jax.random.randint(base_key, (SSM_HEADS, ITEM_COUNT), 1, 4, jnp.int32)
    spike_index = jax.random.randint(layout_seed, (2,), 0, ITEM_COUNT, jnp.int32)
    element_indices = jnp.arange(ITEM_COUNT, dtype=jnp.int32)
    target_classes = jnp.where(element_indices[None, :] == spike_index[1], ITEM_COUNT, target_classes)
    target_classes = jnp.where(element_indices[None, :] == spike_index[0], 2 * ITEM_COUNT, target_classes)
    return target_classes.astype(jnp.int32)


def base_rows(key):
    return jnp.clip(jax.random.normal(key, (ITEM_COUNT, HEADS * HD), jnp.float32), -5.0, 5.0)


def draw_queries(key, part):
    values = base_rows(jax.random.fold_in(key, 202))
    return values.astype(jnp.bfloat16)


def draw_keys(key, part):
    values = base_rows(jax.random.fold_in(key, 203))
    return values.astype(jnp.bfloat16)


def shard_levels(key, dims, split, least, top_value):
    def one(position, parts):
        steps = jax.random.uniform(jax.random.fold_in(jax.random.fold_in(key, 6), position), (parts,), jnp.float32, least / len(split), top_value / len(split))
        return jnp.repeat(jnp.exp(steps), dims[position] // parts).reshape((-1,) + (1,) * (len(dims) - position - 1))

    level = one(*split[0])
    for cut in split[1:]:
        level = level * one(*cut)
    return level


def centred(rng, dims, width, reach, shards=(), kind=jnp.bfloat16):
    drawn = width * jax.random.normal(rng, dims, jnp.float32)
    if shards:
        drawn = drawn * shard_levels(rng, dims, shards, -0.22, 0.18)
    return jnp.clip(drawn, -reach, reach).astype(kind)


def setup_inputs(seed: int = 0) -> dict:
    key_list = jax.random.split(jax.random.key(seed), 11)
    mixer_input = draw_mixer_input(jax.random.fold_in(key_list[10], 71), 0)
    gate_input = centred(key_list[1], (ITEM_COUNT, D_INNER), 1.0, 5.0, ((0, 8), (1, 4)))
    b_proj = centred(key_list[2], (ITEM_COUNT, D_STATE), 0.0884, 0.5, ((0, 8),))
    c_proj = centred(key_list[3], (ITEM_COUNT, D_STATE), 0.0884, 0.5, ((0, 8),))
    decay_codes = draw_decay_codes(jax.random.fold_in(key_list[10], 71), 0)
    decay_rates = draw_decay_rates(jax.random.fold_in(key_list[10], 71), 0)
    skip_gain = jnp.clip(0.5 + 1.0 * jax.random.uniform(key_list[6], (SSM_HEADS,), jnp.float32) ** shard_levels(key_list[6], (SSM_HEADS,), ((0, 4),), -0.2, 0.2), 0.5, 1.5)
    norm_gain = jnp.clip(1.0 + 0.1 * jax.random.normal(key_list[7], (D_INNER,), jnp.float32), 0.5, 1.5)
    queries = draw_queries(jax.random.fold_in(key_list[10], 71), 0)
    keys = draw_keys(jax.random.fold_in(key_list[10], 71), 0)
    return {"mixer_input": mixer_input, "gate_input": gate_input, "b_proj": b_proj, "c_proj": c_proj, "decay_codes": decay_codes, "decay_rates": decay_rates, "skip_gain": skip_gain, "norm_gain": norm_gain, "queries": queries, "keys": keys}


HIGH = lax.Precision.HIGHEST
NEG = -1e+30

def block_step(state_carry, inputs):
    x_block, b_block, c_block, decay_block = inputs
    running = jnp.cumsum(decay_block, axis=1)
    span = decay_block.shape[1]
    causal = jnp.arange(span, dtype=jnp.int32)[:, None] >= jnp.arange(span, dtype=jnp.int32)[None, :]
    log_gaps = jnp.where(causal[None, :, :], running[:, :, None] - running[:, None, :], NEG)
    decays = jnp.exp(log_gaps)
    match_strength = jnp.dot(c_block, b_block.T, preferred_element_type=jnp.float32)
    x_float = x_block.astype(jnp.float32)
    within = jnp.einsum('hts,shp->thp', decays * match_strength[None, :, :], x_float, precision=HIGH)
    c_float = c_block.astype(jnp.float32)
    carried = jnp.exp(running).T[:, :, None] * jnp.einsum('tn,hnp->thp', c_float, state_carry, precision=HIGH)
    to_end = jnp.exp(running[:, -1:] - running)
    updated_state = jnp.exp(running[:, -1])[:, None, None] * state_carry + jnp.einsum('hs,sn,shp->hnp', to_end, b_block.astype(jnp.float32), x_float, precision=HIGH)
    return (updated_state, within + carried)

def reference(mixer_input, gate_input, b_proj, c_proj, decay_codes, decay_rates, skip_gain, norm_gain, queries, keys):
    length = mixer_input.shape[0]
    ssm_heads = decay_rates.shape[0]
    block_count = length // BLOCK
    log_decay = -decay_rates[:, None] * decay_codes.astype(jnp.float32)
    x_blocks = mixer_input.reshape(block_count, BLOCK, ssm_heads, CHANNELS_PER_HD)
    b_blocks = b_proj.reshape(block_count, BLOCK, D_STATE)
    c_blocks = c_proj.reshape(block_count, BLOCK, D_STATE)
    decay_blocks = log_decay.reshape(ssm_heads, block_count, BLOCK).transpose(1, 0, 2)
    initial = jnp.zeros((ssm_heads, D_STATE, CHANNELS_PER_HD), jnp.float32)
    _, y_blocks = lax.scan(block_step, initial, (x_blocks, b_blocks, c_blocks, decay_blocks))
    x_float = mixer_input.reshape(length, ssm_heads, CHANNELS_PER_HD).astype(jnp.float32)
    ssm_out = y_blocks.reshape(length, ssm_heads, CHANNELS_PER_HD) + skip_gain[None, :, None] * x_float
    ssm_out = ssm_out.reshape(length, ssm_heads * CHANNELS_PER_HD)
    gated = ssm_out * jax.nn.silu(gate_input.astype(jnp.float32))
    mean_square = lax.optimization_barrier(jnp.mean(gated * gated, axis=1, keepdims=True))
    mamba_out = (gated * lax.rsqrt(mean_square + 1e-05) * norm_gain[None, :]).astype(jnp.bfloat16)
    score_scale = 1.0 / math.sqrt(HD)
    query_groups = queries.reshape(length, HEADS, HD).transpose(1, 0, 2)
    k_heads = keys.reshape(length, HEADS, HD).transpose(1, 0, 2)
    v_heads = mamba_out.reshape(length, HEADS, HD).transpose(1, 0, 2)
    query_rows = math.gcd(length, 512)

    def one_head(operands):
        q_head, k_head, v_head = operands

        def one_block(row_start):
            q_block = lax.dynamic_slice_in_dim(q_head, row_start, query_rows, 0)
            scores = jnp.dot(q_block, k_head.T, preferred_element_type=jnp.float32) * score_scale
            q_pos = row_start + jnp.arange(query_rows, dtype=jnp.int32)
            k_pos = jnp.arange(length, dtype=jnp.int32)
            causal = k_pos[None, :] <= q_pos[:, None]
            scores = jnp.where(causal, scores, NEG)
            row_top = lax.optimization_barrier(jnp.max(scores, axis=1, keepdims=True))
            weights = jnp.where(causal, jnp.exp(scores - row_top), 0.0)
            denominator = lax.optimization_barrier(jnp.sum(weights, axis=1, keepdims=True))
            numerator = jnp.dot(weights.astype(jnp.bfloat16), v_head, preferred_element_type=jnp.float32)
            return (numerator / denominator).astype(jnp.bfloat16)
        starts = jnp.arange(0, length, query_rows, dtype=jnp.int32)
        return lax.map(one_block, starts).reshape(length, HD)
    attended = lax.map(one_head, (query_groups, k_heads, v_heads))
    attn_out = attended.transpose(1, 0, 2).reshape(length, HEADS * HD)
    return (mamba_out, attn_out)
```

```python
import functools
import math

import jax
import jax.numpy as jnp
from jax import lax
from jax.experimental import pallas as pl
from jax.experimental.pallas import tpu as pltpu
from jax.sharding import PartitionSpec as P

HD = 128
CHANNELS_PER_HD = 64
BLOCK = 256


HIGH = lax.Precision.HIGHEST
NEG = -1e30
LOG2E = 1.4426950408889634
MIB = 1 << 20


VMEM = pl.BlockSpec(memory_space=pltpu.VMEM)
SMEM = pl.BlockSpec(memory_space=pltpu.SMEM)


def call(body, outs, args, scalars, scratch=(), flops=0, moved=0, exps=0, limit=16 * MIB):
    return pl.pallas_call(
        body,
        out_shape=outs,
        in_specs=[SMEM] * scalars + [VMEM] * (len(args) - scalars),
        out_specs=jax.tree.map(lambda _: VMEM, outs),
        scratch_shapes=list(scratch),
        compiler_params=pltpu.CompilerParams(vmem_limit_bytes=limit),
        cost_estimate=pl.CostEstimate(flops=flops, bytes_accessed=moved, transcendentals=exps),
    )(*args)


def nt(a, b):
    return lax.dot_general(a, b, (((1,), (1,)), ((), ())), preferred_element_type=jnp.float32)


def nn(a, b):
    return jnp.dot(a, b, preferred_element_type=jnp.float32)


def step_counts(codes):
    heads, rows = codes.shape
    r = lax.broadcasted_iota(jnp.int32, (rows, rows), 0)
    s = lax.broadcasted_iota(jnp.int32, (rows, rows), 1)
    upper = (r <= s).astype(jnp.float32).astype(jnp.bfloat16)
    lower = (s <= r).astype(jnp.float32).astype(jnp.bfloat16)
    high = lax.shift_right_logical(codes, 7).astype(jnp.float32).astype(jnp.bfloat16)
    low = (codes & 127).astype(jnp.float32).astype(jnp.bfloat16)
    return (
        128.0 * nn(high, upper) + nn(low, upper),
        128.0 * nt(lower, high) + nt(lower, low),
    )


def left_lanes(rows):
    return lax.broadcasted_iota(jnp.int32, (rows, HD), 1) < CHANNELS_PER_HD


def lanes_of(block):
    return pl.ds(pl.multiple_of(block * HD, HD), HD)


def rotated(me, k, n):
    return lax.rem(me + k, n)


def qk_kernel(n, me_ref, q_ref, k_ref, *outs):
    rows = q_ref.shape[0]
    me = me_ref[0]
    for k in range(n):
        cols = lanes_of(rotated(me, k, n))
        outs[k][pl.ds(0, rows), :] = q_ref[:, cols]
        outs[k][pl.ds(rows, rows), :] = k_ref[:, cols]


def state_kernel(n, me_ref, rates_ref, x_ref, b_ref, codes_ref, *rest):
    outs, held = rest[:n], rest[n]
    rows = x_ref.shape[0]
    me = me_ref[0]
    _, counts = step_counts(codes_ref[...])
    b_turned = b_ref[...].astype(jnp.float32).T.astype(jnp.bfloat16)
    left = left_lanes(rows)
    part = lax.broadcasted_iota(jnp.int32, (16, HD), 0)
    for pair in range(n):
        ends = []
        totals = []
        for h in (2 * pair, 2 * pair + 1):
            column = counts[:, h : h + 1]
            total = counts[rows - 1 : rows, h : h + 1]
            totals.append(total)
            ends.append(jnp.exp2((total - column) * (-rates_ref[h] * LOG2E)))
        weight = jnp.where(left, ends[0], ends[1])
        x = x_ref[:, pair * HD : (pair + 1) * HD].astype(jnp.float32)
        held[pair, pl.ds(0, HD), :] = nn(b_turned, (x * weight).astype(jnp.bfloat16)).astype(
            jnp.bfloat16
        )
        total = jnp.where(left_lanes(16), totals[0], totals[1]).astype(jnp.int32)
        parts = jnp.where(
            part == 0,
            lax.shift_right_logical(total, 16),
            jnp.where(
                part == 1,
                lax.shift_right_logical(total, 8) & 255,
                jnp.where(part == 2, total & 255, 0),
            ),
        )
        held[pair, pl.ds(HD, 16), :] = parts.astype(jnp.float32).astype(jnp.bfloat16)
    for k in range(n):
        outs[k][...] = held[rotated(me, k, n)]


def carry_kernel(n, me_ref, rates_ref, *rest):
    ins, outs, held, ahead = rest[:n], rest[n : 2 * n], rest[2 * n], rest[2 * n + 1]
    me = me_ref[0]
    for k in range(n):
        held[rotated(me, n - k, n)] = ins[k][...]
    rate = jnp.where(left_lanes(1), rates_ref[2 * me], rates_ref[2 * me + 1])
    state = jnp.zeros((HD, HD), jnp.float32)
    for r in range(n):
        ahead[r] = state.astype(jnp.bfloat16)
        parts = held[r, pl.ds(HD, 16), :].astype(jnp.float32)
        total = 65536.0 * parts[0:1] + 256.0 * parts[1:2] + parts[2:3]
        decay = jnp.exp2(total * (-rate * LOG2E))
        state = decay * state + held[r, pl.ds(0, HD), :].astype(jnp.float32)
    for k in range(n):
        outs[k][...] = ahead[rotated(me, k, n)]


def within_kernel(
    n, rates_ref, skip_ref, x_ref, gate_ref, b_ref, c_ref, codes_ref, own_ref, lead_ref
):
    rows = x_ref.shape[0]
    across, down = step_counts(codes_ref[...])
    t = lax.broadcasted_iota(jnp.int32, (rows, rows), 0)
    s = lax.broadcasted_iota(jnp.int32, (rows, rows), 1)
    match = jnp.where(s <= t, nt(c_ref[...], b_ref[...]), 0.0)
    left = left_lanes(rows)
    for pair in range(n):
        cols = slice(pair * HD, (pair + 1) * HD)
        x = x_ref[:, cols]
        ys = []
        leads = []
        for h in (2 * pair, 2 * pair + 1):
            slope = -rates_ref[h] * LOG2E
            gap = jnp.maximum(down[:, h : h + 1] - across[h : h + 1, :], 0.0)
            ys.append(nn((jnp.exp2(gap * slope) * match).astype(jnp.bfloat16), x))
            leads.append(jnp.exp2(down[:, h : h + 1] * slope))
        skip = jnp.where(left_lanes(1), skip_ref[2 * pair], skip_ref[2 * pair + 1])
        gate = gate_ref[:, cols].astype(jnp.float32)
        gate = gate / (1.0 + jnp.exp(-gate))
        own_ref[:, cols] = (jnp.where(left, ys[0], ys[1]) + skip * x.astype(jnp.float32)) * gate
        lead_ref[:, cols] = jnp.where(left, leads[0], leads[1]) * gate


def gated_kernel(n, me_ref, own_ref, lead_ref, c_ref, *rest):
    states, gated_ref, squares_ref, outs = rest[:n], rest[n], rest[n + 1], rest[n + 2 :]
    me = me_ref[0]
    ones = jnp.ones((8, HD), jnp.bfloat16)
    total = jnp.zeros(squares_ref.shape, jnp.float32)
    for k in range(n):
        cols = lanes_of(rotated(me, n - k, n))
        gated = own_ref[:, cols] + lead_ref[:, cols] * nn(c_ref[...], states[k][...])
        gated_ref[:, cols] = gated
        outs[(n - k) % n][...] = gated.astype(jnp.bfloat16)
        square = gated * gated
        high = square.astype(jnp.bfloat16)
        low = (square - high.astype(jnp.float32)).astype(jnp.bfloat16)
        total = total + nt(ones, high) + nt(ones, low)
    squares_ref[...] = total


def turned(row):
    size = row.shape[1]
    r = lax.broadcasted_iota(jnp.int32, (size, size), 0)
    s = lax.broadcasted_iota(jnp.int32, (size, size), 1)
    return jnp.sum(jnp.where(r == s, jnp.broadcast_to(row, (size, size)), 0.0), axis=1, keepdims=True)


def norm_kernel(m, channels, gated_ref, gain_ref, *rest):
    squares, out_ref, factor_ref = rest[:m], rest[m], rest[m + 1]
    total = squares[0][...]
    for part in squares[1:]:
        total = total + part[...]
    factor = lax.rsqrt(total / channels + 1e-05)
    factor_ref[...] = factor
    column = turned(factor[0:1])
    for at in range(0, gated_ref.shape[1], HD):
        cols = slice(at, at + HD)
        out_ref[:, cols] = (gated_ref[:, cols] * column * gain_ref[:, cols]).astype(jnp.bfloat16)


def weights_kernel(n, me_ref, *rest):
    ins, out_ref, q_ref, k_ref = rest[:n], rest[n], rest[n + 1], rest[n + 2]
    rows = ins[0].shape[0] // 2
    me = me_ref[0]
    for k in range(n):
        at = pl.ds(pl.multiple_of(rotated(me, n - k, n) * rows, rows), rows)
        q_ref[at, :] = ins[k][pl.ds(0, rows), :]
        k_ref[at, :] = ins[k][pl.ds(rows, rows), :]
    scale = LOG2E / math.sqrt(HD)
    half = rows // 2
    for i in range(2 * n):
        seen = (i // 2) * rows
        q = q_ref[pl.ds(i * half, half), :]
        t = lax.broadcasted_iota(jnp.int32, (half, rows), 0) + (i % 2) * half
        s = lax.broadcasted_iota(jnp.int32, (half, rows), 1)
        blocks = [nt(q, k_ref[pl.ds(at, rows), :]) for at in range(0, seen, rows)]
        blocks.append(jnp.where(s <= t, nt(q, k_ref[pl.ds(seen, rows), :]), NEG))
        top = functools.reduce(jnp.maximum, blocks)
        top = jnp.max(top, axis=1, keepdims=True) * scale
        blocks = [jnp.exp2(block * scale - top) for block in blocks]
        total = jnp.sum(functools.reduce(jnp.add, blocks), axis=1, keepdims=True)
        inverse = 1.0 / total
        for j, block in enumerate(blocks):
            out_ref[pl.ds(i * half, half), pl.ds(j * rows, rows)] = (block * inverse).astype(
                jnp.bfloat16
            )


def values_kernel(n, me_ref, weights_ref, gain_ref, *rest):
    ins, factors, outs = rest[:n], rest[n : 2 * n], rest[2 * n : 3 * n]
    v_ref, o_ref = rest[3 * n :]
    rows = ins[0].shape[0]
    me = me_ref[0]
    gain = gain_ref[:, lanes_of(me)]
    for k in range(n):
        at = pl.ds(pl.multiple_of(rotated(me, n - k, n) * rows, rows), rows)
        column = turned(factors[k][0:1, :])
        v_ref[at, :] = (ins[k][...].astype(jnp.float32) * column * gain).astype(jnp.bfloat16)
    for i in range(n):
        seen = (i + 1) * rows
        o_ref[i] = nn(
            weights_ref[pl.ds(i * rows, rows), pl.ds(0, seen)], v_ref[pl.ds(0, seen), :]
        ).astype(jnp.bfloat16)
    for k in range(n):
        outs[k][...] = o_ref[rotated(me, k, n)]


def join_kernel(n, me_ref, *rest):
    me = me_ref[0]
    for k in range(n):
        rest[n][:, lanes_of(rotated(me, n - k, n))] = rest[k][...]


def exchange(parts, axis):
    n = len(parts)
    return [parts[0]] + [
        lax.ppermute(parts[k], axis, [(i, (i + k) % n) for i in range(n)]) for k in range(1, n)
    ]


def one_head_each(
    mixer_input,
    gate_input,
    b_proj,
    c_proj,
    decay_codes,
    decay_rates,
    skip_gain,
    norm_gain,
    queries,
    keys,
):
    n, m = lax.axis_size("seq"), lax.axis_size("head")
    rows, width = mixer_input.shape
    me = lax.axis_index("seq").astype(jnp.int32).reshape(1)
    gain = norm_gain.reshape(1, width)
    shape = jax.ShapeDtypeStruct
    bf16, f32 = jnp.bfloat16, jnp.float32
    chunk = shape((rows, HD), bf16)

    states = call(
        functools.partial(state_kernel, n),
        [shape((HD + 16, HD), bf16)] * n,
        (me, decay_rates, mixer_input, b_proj, decay_codes),
        2,
        [pltpu.VMEM((n, HD + 16, HD), bf16)],
        flops=2 * rows * HD * width,
        moved=3 * rows * width,
    )
    states = exchange(states, "seq")
    qk = call(
        functools.partial(qk_kernel, n),
        [shape((2 * rows, HD), bf16)] * n,
        (me, queries, keys),
        1,
        moved=8 * rows * width,
    )
    qk = exchange(qk, "seq")
    own, lead = call(
        functools.partial(within_kernel, n),
        [shape((rows, width), f32)] * 2,
        (decay_rates, skip_gain, mixer_input, gate_input, b_proj, c_proj, decay_codes),
        2,
        flops=4 * rows * rows * width,
        moved=12 * rows * width,
        exps=2 * n * rows * rows,
    )
    ahead = call(
        functools.partial(carry_kernel, n),
        [shape((HD, HD), bf16)] * n,
        (me, decay_rates, *states),
        2,
        [pltpu.VMEM((n, HD + 16, HD), bf16), pltpu.VMEM((n, HD, HD), bf16)],
        flops=4 * n * HD * HD,
        moved=4 * n * HD * HD,
    )
    ahead = exchange(ahead, "seq")
    gated, squares, *values = call(
        functools.partial(gated_kernel, n),
        [shape((rows, width), f32), shape((8, rows), f32)] + [chunk] * n,
        (me, own, lead, c_proj, *ahead),
        1,
        flops=4 * rows * HD * width,
        moved=14 * rows * width,
    )
    values = exchange(values, "seq")
    squares = exchange([squares] * m, "head")
    mamba_out, factor = call(
        functools.partial(norm_kernel, m, width * m),
        [shape((rows, width), bf16), shape((8, rows), f32)],
        (gated, gain, *squares),
        0,
        flops=4 * rows * width,
        moved=6 * rows * width,
    )
    factors = exchange([factor] * n, "seq")
    weights = call(
        functools.partial(weights_kernel, n),
        shape((n * rows, n * rows), bf16),
        (me, *qk),
        1,
        [pltpu.VMEM((n * rows, HD), bf16), pltpu.VMEM((n * rows, HD), bf16)],
        flops=n * n * rows * rows * HD,
        moved=2 * n * n * rows * rows,
        exps=n * n * rows * rows // 2,
        limit=24 * MIB,
    )
    results = call(
        functools.partial(values_kernel, n),
        [chunk] * n,
        (me, weights, gain, *values, *factors),
        1,
        [pltpu.VMEM((n * rows, HD), bf16), pltpu.VMEM((n, rows, HD), bf16)],
        flops=n * n * rows * rows * HD,
        moved=2 * n * n * rows * rows,
    )
    results = exchange(results, "seq")
    attn_out = call(
        functools.partial(join_kernel, n),
        shape((rows, width), bf16),
        (me, *results),
        1,
        moved=4 * rows * width,
    )
    return (mamba_out, attn_out)


def running_sum(log_decay):
    span = log_decay.shape[1]
    at = jnp.arange(span, dtype=jnp.int32)
    earlier = (at[:, None] <= at[None, :]).astype(jnp.float32)
    return jnp.dot(log_decay, earlier, precision=HIGH)


def carried_in(array, axis, combine, identity):
    devices, mine = (lax.axis_size(axis), lax.axis_index(axis))
    everything = jax.tree.map(
        lambda part, kind: lax.all_gather(part.astype(kind), axis),
        array,
        (jnp.bfloat16, jnp.bfloat16),
    )
    start = jax.tree.map(
        lambda part, zero: jnp.broadcast_to(jnp.asarray(zero, part.dtype), part.shape),
        array,
        identity,
    )

    def hop(k, before):
        reached = k < mine
        new = combine(
            before, jax.tree.map(lambda part, own: part[k].astype(own.dtype), everything, array)
        )
        return jax.tree.map(lambda a, b: jnp.where(reached, a, b), new, before)

    return lax.fori_loop(0, devices, hop, start)


def block_step(state_carry, inputs):
    x_block, b_block, c_block, decay_block = inputs
    running = running_sum(decay_block)
    span = decay_block.shape[1]
    causal = (
        jnp.arange(span, dtype=jnp.int32)[:, None] >= jnp.arange(span, dtype=jnp.int32)[None, :]
    )
    log_gaps = jnp.where(causal[None, :, :], running[:, :, None] - running[:, None, :], NEG)
    decays = jnp.exp(log_gaps)
    match_strength = jnp.dot(c_block, b_block.T, preferred_element_type=jnp.float32)
    x_float = x_block.astype(jnp.float32)
    within = jnp.einsum(
        "hts,shp->thp", decays * match_strength[None, :, :], x_float, precision=HIGH
    )
    c_float = c_block.astype(jnp.float32)
    carried = jnp.exp(running).T[:, :, None] * jnp.einsum(
        "tn,hnp->thp", c_float, state_carry, precision=HIGH
    )
    to_end = jnp.exp(running[:, -1:] - running)
    updated_state = jnp.exp(running[:, -1])[:, None, None] * state_carry + jnp.einsum(
        "hs,sn,shp->hnp", to_end, b_block.astype(jnp.float32), x_float, precision=HIGH
    )
    return (updated_state, within + carried)


def local_scan(x_local, b_local, c_local, log_decay):
    tok_rows = x_local.shape[0]
    heads_local = log_decay.shape[0]
    block_count = tok_rows // BLOCK
    x_blocks = x_local.reshape(block_count, BLOCK, heads_local, CHANNELS_PER_HD)
    b_blocks = b_local.reshape(block_count, BLOCK, b_local.shape[1])
    c_blocks = c_local.reshape(block_count, BLOCK, c_local.shape[1])
    decay_blocks = log_decay.reshape(heads_local, block_count, BLOCK).transpose(1, 0, 2)
    initial = jnp.zeros((heads_local, b_local.shape[1], CHANNELS_PER_HD), jnp.float32)
    final_state, y_blocks = lax.scan(
        block_step, initial, (x_blocks, b_blocks, c_blocks, decay_blocks)
    )
    return (final_state, y_blocks.reshape(tok_rows, heads_local, CHANNELS_PER_HD))


def masked_scores(q_rows, q_pos, k_rows, k_pos):
    score_scale = 1.0 / math.sqrt(k_rows.shape[-1])
    scores = (
        jnp.einsum("qhd,khd->hqk", q_rows, k_rows, preferred_element_type=jnp.float32) * score_scale
    )
    visible = k_pos[None, None, :] <= q_pos[None, :, None]
    return (jnp.where(visible, scores, NEG), visible)


def online_update(group_state, q_rows, q_pos, k_rows, v_rows, k_pos):
    row_top, row_total, weighted_sum = group_state
    scores, visible = masked_scores(q_rows, q_pos, k_rows, k_pos)
    new_top = jnp.maximum(row_top, jnp.max(scores, axis=2))
    rescale = jnp.exp(row_top - new_top)
    weights = jnp.where(visible, jnp.exp(scores - new_top[:, :, None]), 0.0)
    row_total = row_total * rescale + jnp.sum(weights, axis=2)
    weighted_sum = weighted_sum * rescale[:, :, None] + jnp.einsum(
        "hqk,khd->hqd", weights.astype(jnp.bfloat16), v_rows, preferred_element_type=jnp.float32
    )
    return (new_top, row_total, weighted_sum)


def when_visible(state_update, group_state, q_pos, key_offset):
    return lax.cond(key_offset > q_pos[-1], lambda held: held, state_update, group_state)


def gathered(
    mixer_input,
    gate_input,
    b_proj,
    c_proj,
    decay_codes,
    decay_rates,
    skip_gain,
    norm_gain,
    queries,
    keys,
):
    tok_rows = mixer_input.shape[0]
    heads_local = decay_rates.shape[0]
    heads_att = queries.shape[1] // HD
    seq_rank = lax.axis_index("seq")
    own_positions = seq_rank * tok_rows + jnp.arange(tok_rows, dtype=jnp.int32)
    groups = [(queries, own_positions)]
    groups = [(q_rows.reshape(q_rows.shape[0], heads_att, HD), q_pos) for q_rows, q_pos in groups]
    log_decay = -decay_rates[:, None] * decay_codes.astype(jnp.float32)
    local_state, y_local = local_scan(mixer_input, b_proj, c_proj, log_decay)
    total_log = jnp.sum(log_decay, axis=1)

    def combine(earlier, later):
        return (earlier[0] + later[0], jnp.exp(later[0])[:, None, None] * earlier[1] + later[1])

    identity = (jnp.zeros_like(total_log), jnp.zeros_like(local_state))
    _, incoming = carried_in((total_log, local_state), "seq", combine, identity)
    running = running_sum(log_decay)
    carried = jnp.einsum("tn,hnp->thp", c_proj.astype(jnp.float32), incoming, precision=HIGH)
    carried = carried * jnp.exp(running).T[:, :, None]
    x_float = mixer_input.reshape(tok_rows, heads_local, CHANNELS_PER_HD).astype(jnp.float32)
    ssm_out = (y_local + carried + skip_gain[None, :, None] * x_float).reshape(
        tok_rows, heads_local * CHANNELS_PER_HD
    )
    gated = ssm_out * jax.nn.silu(gate_input.astype(jnp.float32))
    squares = lax.psum(jnp.sum(gated * gated, axis=1), "head")
    channels = gated.shape[1] * lax.axis_size("head")
    mamba_out = (
        gated * lax.rsqrt(squares / channels + 1e-05)[:, None] * norm_gain[None, :]
    ).astype(jnp.bfloat16)
    initial = tuple(
        (
            (
                jnp.full((heads_att, q_pos.shape[0]), NEG, jnp.float32),
                jnp.zeros((heads_att, q_pos.shape[0]), jnp.float32),
                jnp.zeros((heads_att, q_pos.shape[0], HD), jnp.float32),
            )
            for _, q_pos in groups
        )
    )
    states = initial
    k_piece = lax.all_gather(keys, "seq", axis=0, tiled=True)
    v_piece = lax.all_gather(mamba_out, "seq", axis=0, tiled=True)
    row_count = k_piece.shape[0]
    block_rows = math.gcd(row_count, 512)

    def one_block(block_id, states):
        key_offset = block_id * block_rows
        k_rows = lax.dynamic_slice_in_dim(k_piece, block_id * block_rows, block_rows, 0).reshape(
            block_rows, heads_att, HD
        )
        v_rows = lax.dynamic_slice_in_dim(v_piece, block_id * block_rows, block_rows, 0).reshape(
            block_rows, heads_att, HD
        )
        k_pos = key_offset + jnp.arange(block_rows, dtype=jnp.int32)
        return tuple(
            (
                when_visible(
                    functools.partial(
                        online_update,
                        q_rows=group[0],
                        q_pos=group[1],
                        k_rows=k_rows,
                        v_rows=v_rows,
                        k_pos=k_pos,
                    ),
                    group_state,
                    group[1],
                    key_offset,
                )
                for group, group_state in zip(groups, states)
            )
        )

    finals = lax.fori_loop(0, row_count // block_rows, one_block, states)
    results = [(group_state[2], group_state[1]) for group_state in finals]
    rows_out = [
        (weighted / totals[:, :, None])
        .transpose(1, 0, 2)
        .reshape(weighted.shape[1], heads_att * HD)
        .astype(jnp.bfloat16)
        for weighted, totals in results
    ]
    attn_out = rows_out[0]
    return (mamba_out, attn_out)


def on_device(mixer_input, gate_input, b_proj, c_proj, decay_codes, *others):
    n = lax.axis_size("seq")
    rows, width = mixer_input.shape
    fits = (
        width == n * HD
        and decay_codes.shape[0] == 2 * n
        and b_proj.shape[1] == HD
        and rows == BLOCK
        and n <= 8
    )
    return (one_head_each if fits else gathered)(
        mixer_input, gate_input, b_proj, c_proj, decay_codes, *others
    )


def solution(mesh):
    in_specs = (
        P("seq", "head"),
        P("seq", "head"),
        P("seq", None),
        P("seq", None),
        P("head", "seq"),
        P("head"),
        P("head"),
        P("head"),
        P("seq", "head"),
        P("seq", "head"),
    )
    out_specs = (P("seq", "head"), P("seq", "head"))
    return jax.shard_map(
        on_device, mesh=mesh, in_specs=in_specs, out_specs=out_specs, check_vma=False
    )
```

```python
import functools
import math

import jax
import jax.numpy as jnp
from jax import lax
from jax.experimental import pallas as pl
from jax.experimental.pallas import tpu as pltpu
from jax.sharding import PartitionSpec as P

HD = 128
CHANNELS_PER_HD = 64
BLOCK = 256


HIGH = lax.Precision.HIGHEST
NEG = -1e30
LOG2E = 1.4426950408889634
MIB = 1 << 20


VMEM = pl.BlockSpec(memory_space=pltpu.VMEM)
SMEM = pl.BlockSpec(memory_space=pltpu.SMEM)
HBM = pl.BlockSpec(memory_space=pltpu.HBM)
ANY = pl.BlockSpec(memory_space=pl.ANY)
CHIPS = 4
WIDE = 2 * HD
PARTS = 16


def call(body, outs, args, spaces, scratch=(), flops=0, moved=0, exps=0, limit=16 * MIB):
    kinds = {"s": SMEM, "h": HBM, "a": ANY, "v": VMEM}
    spaces = spaces + "v" * (len(args) - len(spaces))
    return pl.pallas_call(
        body,
        out_shape=outs,
        in_specs=[kinds[space] for space in spaces],
        out_specs=jax.tree.map(lambda _: VMEM, outs),
        scratch_shapes=list(scratch),
        compiler_params=pltpu.CompilerParams(vmem_limit_bytes=limit),
        cost_estimate=pl.CostEstimate(flops=0, bytes_accessed=0, transcendentals=0),
    )(
        *(
            pltpu.with_memory_space_constraint(arg, pltpu.HBM) if space == "h" else arg
            for arg, space in zip(args, spaces)
        )
    )


def nt(a, b):
    return lax.dot_general(a, b, (((1,), (1,)), ((), ())), preferred_element_type=jnp.float32)


def nn(a, b):
    return jnp.dot(a, b, preferred_element_type=jnp.float32)


def step_counts(codes):
    rows = codes.shape[1]
    r = lax.broadcasted_iota(jnp.int32, (rows, rows), 0)
    s = lax.broadcasted_iota(jnp.int32, (rows, rows), 1)
    upper = (r <= s).astype(jnp.float32).astype(jnp.bfloat16)
    lower = (s <= r).astype(jnp.float32).astype(jnp.bfloat16)
    high = lax.shift_right_logical(codes, 7).astype(jnp.float32).astype(jnp.bfloat16)
    low = (codes & 127).astype(jnp.float32).astype(jnp.bfloat16)
    return (
        128.0 * nn(high, upper) + nn(low, upper),
        128.0 * nt(lower, high) + nt(lower, low),
    )


def left_lanes(rows):
    return lax.broadcasted_iota(jnp.int32, (rows, HD), 1) < CHANNELS_PER_HD


def chip_of(me):
    return lax.shift_right_logical(me, 1)


def around(chip, by):
    return (chip + by) & (CHIPS - 1)


def block_of(index, size):
    return pl.ds(pl.multiple_of(index * size, size), size)


def as_parts(total):
    total = jnp.broadcast_to(total, (PARTS, total.shape[1])).astype(jnp.int32)
    part = lax.broadcasted_iota(jnp.int32, total.shape, 0)
    high = lax.shift_right_logical(total, 16)
    middle = lax.shift_right_logical(total, 8) & 255
    chosen = jnp.where(
        part == 0, high, jnp.where(part == 1, middle, jnp.where(part == 2, total & 255, 0))
    )
    return chosen.astype(jnp.float32).astype(jnp.bfloat16)


def opened(rows):
    rows = rows.astype(jnp.float32)
    total = 65536.0 * rows[HD : HD + 1] + 256.0 * rows[HD + 1 : HD + 2] + rows[HD + 2 : HD + 3]
    return rows[:HD], total


def followed(first, second, slope):
    return jnp.exp2(second[1] * slope) * first[0] + second[0], first[1] + second[1]


def first_kernel(
    me_ref, rates_ref, skip_ref, q_hbm, k_hbm, codes_hbm, b_hbm, x_hbm, c_hbm, gate_hbm, gain_hbm, *rest
):
    qk, state_ref, slope_ref, skips_ref = rest[:CHIPS], *rest[CHIPS : CHIPS + 3]
    codes_ref, b_ref, x_ref, c_ref, gate_ref, gain_ref, sems = rest[CHIPS + 3 :]
    rows = x_ref.shape[0]
    chip = chip_of(me_ref[0])
    pairs = [(codes_hbm, codes_ref), (b_hbm, b_ref), (x_hbm, x_ref)]
    for d in range(CHIPS):
        cols = block_of(around(chip, d), WIDE)
        pairs.append((q_hbm.at[:, cols], qk[d].at[pl.ds(0, rows), :]))
        pairs.append((k_hbm.at[:, cols], qk[d].at[pl.ds(rows, rows), :]))
    pairs += [(c_hbm, c_ref), (gate_hbm, gate_ref), (gain_hbm, gain_ref)]
    copies = [pltpu.make_async_copy(a, b, sems.at[i]) for i, (a, b) in enumerate(pairs)]
    for copy in copies:
        copy.start()
    for pair in range(x_ref.shape[1] // HD):
        cols = slice(pair * HD, (pair + 1) * HD)
        left = left_lanes(8)
        one, two = 2 * pair, 2 * pair + 1
        slope_ref[:, cols] = jnp.where(left, rates_ref[one], rates_ref[two]) * -LOG2E
        skips_ref[:, cols] = jnp.where(left, skip_ref[one], skip_ref[two])
    copies[0].wait()
    _, counts = step_counts(codes_ref[...])
    copies[1].wait()
    b_turned = b_ref[...].astype(jnp.float32).T.astype(jnp.bfloat16)
    left = left_lanes(rows)
    copies[2].wait()
    for pair in range(x_ref.shape[1] // HD):
        cols = slice(pair * HD, (pair + 1) * HD)
        column = jnp.where(left, counts[:, 2 * pair : 2 * pair + 1], counts[:, 2 * pair + 1 : 2 * pair + 2])
        total = column[rows - 1 : rows, :]
        weight = jnp.exp2((total - column) * slope_ref[0:1, cols])
        x = (x_ref[:, cols].astype(jnp.float32) * weight).astype(jnp.bfloat16)
        state_ref[pl.ds(0, HD), cols] = nn(b_turned, x).astype(jnp.bfloat16)
        state_ref[pl.ds(HD, PARTS), cols] = as_parts(total)
    for copy in copies[3:]:
        copy.wait()


def chip_kernel(me_ref, slope_ref, own_ref, other_ref, out_ref):
    core = me_ref[0] & 1
    half = own_ref.shape[1] // 2
    cols = block_of(core, half)
    own, other = own_ref[:, cols], other_ref[:, cols]
    first = opened(jnp.where(core == 0, own, other))
    second = opened(jnp.where(core == 0, other, own))
    state, total = followed(first, second, slope_ref[0:1, cols])
    out_ref[pl.ds(0, HD), :] = state.astype(jnp.bfloat16)
    out_ref[pl.ds(HD, PARTS), :] = as_parts(total)


def two_chips_kernel(me_ref, after_ref, slope_ref, own_ref, other_ref, out_ref):
    me = me_ref[0]
    odd = chip_of(me) & 1
    own, other = own_ref[...], other_ref[...]
    first = opened(jnp.where(odd == 0, own, other))
    second = opened(jnp.where(odd == 0, other, own))
    state, total = followed(first, second, slope_ref[0:1, block_of(me & 1, own.shape[1])])
    out_ref[pl.ds(0, HD), :] = state.astype(jnp.bfloat16)
    out_ref[pl.ds(HD, PARTS), :] = as_parts(total)


def ahead_kernel(me_ref, slope_ref, other_ref, far_ref, out_ref):
    me = me_ref[0]
    odd = chip_of(me) & 1
    near, total = opened(other_ref[...])
    near = jnp.where(odd == 1, near, 0.0)
    total = jnp.where(odd == 1, total, 0.0)
    far, _ = opened(far_ref[...])
    slope = slope_ref[0:1, block_of(me & 1, near.shape[1])]
    out_ref[...] = (jnp.exp2(total * slope) * far + near).astype(jnp.bfloat16)


def within_kernel(slope_ref, skips_ref, codes_ref, b_ref, x_ref, c_ref, gate_ref, own_ref, lead_ref):
    rows = x_ref.shape[0]
    across, down = step_counts(codes_ref[...])
    t = lax.broadcasted_iota(jnp.int32, (rows, rows), 0)
    s = lax.broadcasted_iota(jnp.int32, (rows, rows), 1)
    match = jnp.where(s <= t, nt(c_ref[...], b_ref[...]), 0.0)
    left = left_lanes(rows)
    for pair in range(x_ref.shape[1] // HD):
        cols = slice(pair * HD, (pair + 1) * HD)
        x = x_ref[:, cols]
        ys = []
        leads = []
        for h in (2 * pair, 2 * pair + 1):
            slope = slope_ref[0:1, h * CHANNELS_PER_HD : h * CHANNELS_PER_HD + 1]
            gap = jnp.maximum(down[:, h : h + 1] - across[h : h + 1, :], 0.0)
            ys.append(nn((jnp.exp2(gap * slope) * match).astype(jnp.bfloat16), x))
            leads.append(jnp.exp2(down[:, h : h + 1] * slope))
        gate = gate_ref[:, cols].astype(jnp.float32)
        gate = gate / (1.0 + jnp.exp(-gate))
        given = jnp.where(left, ys[0], ys[1]) + skips_ref[0:1, cols] * x.astype(jnp.float32)
        own_ref[:, cols] = given * gate
        lead_ref[:, cols] = jnp.where(left, leads[0], leads[1]) * gate


def gated_kernel(
    me_ref, slope_ref, local_ref, ahead_ref, other_ref, own_ref, lead_ref, c_ref, gated_ref, squares_ref
):
    core = me_ref[0] & 1
    c = c_ref[...]
    ones = jnp.ones((8, HD), jnp.bfloat16)
    squares = jnp.zeros(squares_ref.shape, jnp.float32)
    half = ahead_ref.shape[1]
    for at in range(0, 2 * half, HD):
        cols, within = slice(at, at + HD), slice(at % half, at % half + HD)
        state = jnp.where(core == at // half, ahead_ref[:, within], other_ref[:, within])
        state = state.astype(jnp.float32)
        later, _ = followed((state, 0.0), opened(local_ref[:, cols]), slope_ref[0:1, cols])
        state = jnp.where(core == 1, later, state).astype(jnp.bfloat16)
        gated = own_ref[:, cols] + lead_ref[:, cols] * nn(c, state)
        gated_ref[:, cols] = gated
        square = gated * gated
        high = square.astype(jnp.bfloat16)
        low = (square - high.astype(jnp.float32)).astype(jnp.bfloat16)
        squares = squares + nt(ones, high) + nt(ones, low)
    squares_ref[...] = squares


def turned(row):
    size = row.shape[1]
    r = lax.broadcasted_iota(jnp.int32, (size, size), 0)
    s = lax.broadcasted_iota(jnp.int32, (size, size), 1)
    return jnp.sum(jnp.where(r == s, jnp.broadcast_to(row, (size, size)), 0.0), axis=1, keepdims=True)


def norm_kernel(channels, me_ref, gain_ref, gated_ref, *rest):
    squares, out_ref, parts = rest[: -1 - CHIPS], rest[-1 - CHIPS], rest[-CHIPS:]
    chip = chip_of(me_ref[0])
    total = squares[0][0:1, :]
    for part in squares[1:]:
        total = total + part[0:1, :]
    column = turned(lax.rsqrt(total / channels + 1e-05))
    for d in range(CHIPS):
        cols = block_of(around(chip, d), WIDE)
        out = (gated_ref[:, cols] * column * gain_ref[:, cols]).astype(jnp.bfloat16)
        parts[d][...] = out
        out_ref[:, cols] = out


def keys_kernel(me_ref, after_ref, *rest):
    chip = chip_of(me_ref[0])
    rows = rest[0].shape[0] // 2
    for d in range(CHIPS):
        rest[CHIPS][block_of(around(chip, CHIPS - d), rows), :] = rest[d][pl.ds(rows, rows), :]


def weights_kernel(me_ref, own_ref, other_ref, *rest):
    ins, out_ref, q_ref = rest[:CHIPS], rest[CHIPS], rest[CHIPS + 1]
    rows = ins[0].shape[0] // 2
    me = me_ref[0]
    chip, core = chip_of(me), me & 1
    for d in range(CHIPS):
        q_ref[block_of(around(chip, CHIPS - d), rows), :] = ins[d][pl.ds(0, rows), :]
    scale = LOG2E / math.sqrt(HD)
    half = rows // 2
    for head in range(2):
        lanes = slice(head * HD, (head + 1) * HD)
        for i in range(2 * CHIPS):
            seen = (i // 2) * rows
            q = q_ref[pl.ds(i * half, half), lanes]
            t = lax.broadcasted_iota(jnp.int32, (half, rows), 0) + (i % 2) * half
            s = lax.broadcasted_iota(jnp.int32, (half, rows), 1)
            blocks = []
            for keys_ref, base, shown in (
                (own_ref, 0, s <= t),
                (other_ref, CHIPS * rows, s < core * rows),
            ):
                for at in range(0, seen, rows):
                    blocks.append((base + at, nt(q, keys_ref[pl.ds(at, rows), lanes])))
                last = nt(q, keys_ref[pl.ds(seen, rows), lanes])
                blocks.append((base + seen, jnp.where(shown, last, NEG)))
            top = functools.reduce(jnp.maximum, [block for _, block in blocks])
            top = jnp.max(top, axis=1, keepdims=True) * scale
            blocks = [(at, jnp.exp2(block * scale - top)) for at, block in blocks]
            total = functools.reduce(jnp.add, [block for _, block in blocks])
            inverse = 1.0 / jnp.sum(total, axis=1, keepdims=True)
            for at, block in blocks:
                out_ref[head, pl.ds(i * half, half), pl.ds(at, rows)] = (block * inverse).astype(
                    jnp.bfloat16
                )


def values_kernel(me_ref, weights_ref, *rest):
    own, other, outs = rest[:CHIPS], rest[CHIPS : 2 * CHIPS], rest[2 * CHIPS : 3 * CHIPS]
    v_ref, o_ref = rest[3 * CHIPS :]
    rows = own[0].shape[0]
    chip = chip_of(me_ref[0])
    for d in range(CHIPS):
        back = around(chip, CHIPS - d)
        v_ref[block_of(back, rows), :] = own[d][...]
        v_ref[block_of(back + CHIPS, rows), :] = other[d][...]
    for i in range(CHIPS):
        at, seen = pl.ds(i * rows, rows), (i + 1) * rows
        for head in range(2):
            lanes = slice(head * HD, (head + 1) * HD)
            total = 0.0
            for base in (0, CHIPS * rows):
                seen_at = pl.ds(base, seen)
                total = total + nn(weights_ref[head, at, seen_at], v_ref[seen_at, lanes])
            o_ref[at, lanes] = total.astype(jnp.bfloat16)
    for d in range(CHIPS):
        outs[d][...] = o_ref[block_of(around(chip, d), rows), :]


def join_kernel(me_ref, *rest):
    chip = chip_of(me_ref[0])
    for d in range(CHIPS):
        rest[CHIPS][:, block_of(around(chip, CHIPS - d), WIDE)] = rest[d][...]


def shifted(part, d):
    n = 2 * CHIPS
    return lax.ppermute(part, "seq", [(i, (i + 2 * d) % n) for i in range(n)])


def exchange(parts):
    return [parts[0]] + [shifted(parts[d], d) for d in range(1, CHIPS)]


def swapped(part):
    return lax.ppermute(part, "seq", [(i, i ^ 1) for i in range(2 * CHIPS)])


def two_heads_each(
    mixer_input,
    gate_input,
    b_proj,
    c_proj,
    decay_codes,
    decay_rates,
    skip_gain,
    norm_gain,
    queries,
    keys,
):
    n, m = lax.axis_size("seq"), lax.axis_size("head")
    rows, width = mixer_input.shape
    heads = decay_codes.shape[0]
    me = lax.axis_index("seq").astype(jnp.int32).reshape(1)
    shape = jax.ShapeDtypeStruct
    bf16, f32 = jnp.bfloat16, jnp.float32
    chunk = shape((rows, WIDE), bf16)
    half_state = shape((HD + PARTS, width // 2), bf16)

    *qk, state, slope, skips, codes, b, x, c, gate, gain = call(
        first_kernel,
        [shape((2 * rows, WIDE), bf16)] * CHIPS
        + [shape((HD + PARTS, width), bf16), shape((8, width), f32), shape((8, width), f32)]
        + [
            shape(decay_codes.shape, jnp.int32),
            shape(b_proj.shape, bf16),
            shape((rows, width), bf16),
            shape(c_proj.shape, bf16),
            shape((rows, width), bf16),
            shape((1, width), f32),
        ],
        (me, decay_rates, skip_gain, queries, keys, decay_codes, b_proj, mixer_input, c_proj)
        + (gate_input, norm_gain.reshape(1, width)),
        "ssshhhhhhhh",
        [pltpu.SemaphoreType.DMA((6 + 2 * CHIPS,))],
        flops=2 * rows * HD * width,
        moved=10 * rows * width,
    )
    other = swapped(state)
    qk = exchange(qk)
    own, lead = call(
        within_kernel,
        [shape((rows, width), f32)] * 2,
        (slope, skips, codes, b, x, c, gate),
        "",
        flops=4 * rows * rows * width,
        moved=12 * rows * width,
        exps=heads * rows * rows,
    )
    small = dict(flops=4 * HD * width, moved=4 * HD * width)
    chip_state = call(chip_kernel, half_state, (me, slope, state, other), "s", **small)
    chip_other = lax.ppermute(chip_state, "seq", [(i, i ^ 2) for i in range(n)])
    two_chips = call(
        two_chips_kernel, half_state, (me, own, slope, chip_state, chip_other), "sa", **small
    )
    far = lax.ppermute(two_chips, "seq", [(i, i + 4) for i in range(n // 2)])
    ahead = call(
        ahead_kernel, shape((HD, width // 2), bf16), (me, slope, chip_other, far), "s", **small
    )
    gated, squares = call(
        gated_kernel,
        [shape((rows, width), f32), shape((8, rows), f32)],
        (me, slope, other, ahead, swapped(ahead), own, lead, c),
        "s",
        flops=4 * rows * HD * width,
        moved=14 * rows * width,
    )
    squares = [squares] + [
        lax.ppermute(squares, "head", [(i, (i + k) % m) for i in range(m)]) for k in range(1, m)
    ]
    mamba_out, *values = call(
        functools.partial(norm_kernel, width * m),
        [shape((rows, width), bf16)] + [chunk] * CHIPS,
        (me, gain, gated, *squares),
        "s",
        flops=4 * rows * width,
        moved=8 * rows * width,
    )
    values = exchange(values)
    other_values = [swapped(part) for part in values]
    own_keys = call(
        keys_kernel,
        shape((CHIPS * rows, WIDE), bf16),
        (me, values[0], *qk),
        "sa",
        moved=4 * rows * width,
    )
    weights = call(
        weights_kernel,
        shape((2, CHIPS * rows, n * rows), bf16),
        (me, own_keys, swapped(own_keys), *qk),
        "s",
        [pltpu.VMEM((CHIPS * rows, WIDE), bf16)],
        flops=n * n * rows * rows * HD,
        moved=2 * n * n * rows * rows,
        exps=n * n * rows * rows // 2,
        limit=24 * MIB,
    )
    results = call(
        values_kernel,
        [chunk] * CHIPS,
        (me, weights, *values, *other_values),
        "s",
        [pltpu.VMEM((n * rows, WIDE), bf16), pltpu.VMEM((CHIPS * rows, WIDE), bf16)],
        flops=n * n * rows * rows * HD,
        moved=2 * n * n * rows * rows,
    )
    attn_out = call(
        join_kernel,
        shape((rows, width), bf16),
        (me, *exchange(results)),
        "s",
        moved=4 * rows * width,
    )
    return (mamba_out, attn_out)


def running_sum(log_decay):
    span = log_decay.shape[1]
    at = jnp.arange(span, dtype=jnp.int32)
    earlier = (at[:, None] <= at[None, :]).astype(jnp.float32)
    return jnp.dot(log_decay, earlier, precision=HIGH)


def carried_in(array, axis, combine, identity):
    devices, mine = (lax.axis_size(axis), lax.axis_index(axis))
    everything = jax.tree.map(
        lambda part, kind: lax.all_gather(part.astype(kind), axis),
        array,
        (jnp.bfloat16, jnp.bfloat16),
    )
    start = jax.tree.map(
        lambda part, zero: jnp.broadcast_to(jnp.asarray(zero, part.dtype), part.shape),
        array,
        identity,
    )

    def hop(k, before):
        reached = k < mine
        new = combine(
            before, jax.tree.map(lambda part, own: part[k].astype(own.dtype), everything, array)
        )
        return jax.tree.map(lambda a, b: jnp.where(reached, a, b), new, before)

    return lax.fori_loop(0, devices, hop, start)


def block_step(state_carry, inputs):
    x_block, b_block, c_block, decay_block = inputs
    running = running_sum(decay_block)
    span = decay_block.shape[1]
    causal = (
        jnp.arange(span, dtype=jnp.int32)[:, None] >= jnp.arange(span, dtype=jnp.int32)[None, :]
    )
    log_gaps = jnp.where(causal[None, :, :], running[:, :, None] - running[:, None, :], NEG)
    decays = jnp.exp(log_gaps)
    match_strength = jnp.dot(c_block, b_block.T, preferred_element_type=jnp.float32)
    x_float = x_block.astype(jnp.float32)
    within = jnp.einsum(
        "hts,shp->thp", decays * match_strength[None, :, :], x_float, precision=HIGH
    )
    c_float = c_block.astype(jnp.float32)
    carried = jnp.exp(running).T[:, :, None] * jnp.einsum(
        "tn,hnp->thp", c_float, state_carry, precision=HIGH
    )
    to_end = jnp.exp(running[:, -1:] - running)
    updated_state = jnp.exp(running[:, -1])[:, None, None] * state_carry + jnp.einsum(
        "hs,sn,shp->hnp", to_end, b_block.astype(jnp.float32), x_float, precision=HIGH
    )
    return (updated_state, within + carried)


def local_scan(x_local, b_local, c_local, log_decay):
    tok_rows = x_local.shape[0]
    heads_local = log_decay.shape[0]
    block_count = tok_rows // BLOCK
    x_blocks = x_local.reshape(block_count, BLOCK, heads_local, CHANNELS_PER_HD)
    b_blocks = b_local.reshape(block_count, BLOCK, b_local.shape[1])
    c_blocks = c_local.reshape(block_count, BLOCK, c_local.shape[1])
    decay_blocks = log_decay.reshape(heads_local, block_count, BLOCK).transpose(1, 0, 2)
    initial = jnp.zeros((heads_local, b_local.shape[1], CHANNELS_PER_HD), jnp.float32)
    final_state, y_blocks = lax.scan(
        block_step, initial, (x_blocks, b_blocks, c_blocks, decay_blocks)
    )
    return (final_state, y_blocks.reshape(tok_rows, heads_local, CHANNELS_PER_HD))


def masked_scores(q_rows, q_pos, k_rows, k_pos):
    score_scale = 1.0 / math.sqrt(k_rows.shape[-1])
    scores = (
        jnp.einsum("qhd,khd->hqk", q_rows, k_rows, preferred_element_type=jnp.float32) * score_scale
    )
    visible = k_pos[None, None, :] <= q_pos[None, :, None]
    return (jnp.where(visible, scores, NEG), visible)


def online_update(group_state, q_rows, q_pos, k_rows, v_rows, k_pos):
    row_top, row_total, weighted_sum = group_state
    scores, visible = masked_scores(q_rows, q_pos, k_rows, k_pos)
    new_top = jnp.maximum(row_top, jnp.max(scores, axis=2))
    rescale = jnp.exp(row_top - new_top)
    weights = jnp.where(visible, jnp.exp(scores - new_top[:, :, None]), 0.0)
    row_total = row_total * rescale + jnp.sum(weights, axis=2)
    weighted_sum = weighted_sum * rescale[:, :, None] + jnp.einsum(
        "hqk,khd->hqd", weights.astype(jnp.bfloat16), v_rows, preferred_element_type=jnp.float32
    )
    return (new_top, row_total, weighted_sum)


def when_visible(state_update, group_state, q_pos, key_offset):
    return lax.cond(key_offset > q_pos[-1], lambda held: held, state_update, group_state)


def gathered(
    mixer_input,
    gate_input,
    b_proj,
    c_proj,
    decay_codes,
    decay_rates,
    skip_gain,
    norm_gain,
    queries,
    keys,
):
    tok_rows = mixer_input.shape[0]
    heads_local = decay_rates.shape[0]
    heads_att = queries.shape[1] // HD
    seq_rank = lax.axis_index("seq")
    own_positions = seq_rank * tok_rows + jnp.arange(tok_rows, dtype=jnp.int32)
    groups = [(queries, own_positions)]
    groups = [(q_rows.reshape(q_rows.shape[0], heads_att, HD), q_pos) for q_rows, q_pos in groups]
    log_decay = -decay_rates[:, None] * decay_codes.astype(jnp.float32)
    local_state, y_local = local_scan(mixer_input, b_proj, c_proj, log_decay)
    total_log = jnp.sum(log_decay, axis=1)

    def combine(earlier, later):
        return (earlier[0] + later[0], jnp.exp(later[0])[:, None, None] * earlier[1] + later[1])

    identity = (jnp.zeros_like(total_log), jnp.zeros_like(local_state))
    _, incoming = carried_in((total_log, local_state), "seq", combine, identity)
    running = running_sum(log_decay)
    carried = jnp.einsum("tn,hnp->thp", c_proj.astype(jnp.float32), incoming, precision=HIGH)
    carried = carried * jnp.exp(running).T[:, :, None]
    x_float = mixer_input.reshape(tok_rows, heads_local, CHANNELS_PER_HD).astype(jnp.float32)
    ssm_out = (y_local + carried + skip_gain[None, :, None] * x_float).reshape(
        tok_rows, heads_local * CHANNELS_PER_HD
    )
    gated = ssm_out * jax.nn.silu(gate_input.astype(jnp.float32))
    squares = lax.psum(jnp.sum(gated * gated, axis=1), "head")
    channels = gated.shape[1] * lax.axis_size("head")
    mamba_out = (
        gated * lax.rsqrt(squares / channels + 1e-05)[:, None] * norm_gain[None, :]
    ).astype(jnp.bfloat16)
    initial = tuple(
        (
            (
                jnp.full((heads_att, q_pos.shape[0]), NEG, jnp.float32),
                jnp.zeros((heads_att, q_pos.shape[0]), jnp.float32),
                jnp.zeros((heads_att, q_pos.shape[0], HD), jnp.float32),
            )
            for _, q_pos in groups
        )
    )
    states = initial
    k_piece = lax.all_gather(keys, "seq", axis=0, tiled=True)
    v_piece = lax.all_gather(mamba_out, "seq", axis=0, tiled=True)
    row_count = k_piece.shape[0]
    block_rows = math.gcd(row_count, 512)

    def one_block(block_id, states):
        key_offset = block_id * block_rows
        k_rows = lax.dynamic_slice_in_dim(k_piece, block_id * block_rows, block_rows, 0).reshape(
            block_rows, heads_att, HD
        )
        v_rows = lax.dynamic_slice_in_dim(v_piece, block_id * block_rows, block_rows, 0).reshape(
            block_rows, heads_att, HD
        )
        k_pos = key_offset + jnp.arange(block_rows, dtype=jnp.int32)
        return tuple(
            (
                when_visible(
                    functools.partial(
                        online_update,
                        q_rows=group[0],
                        q_pos=group[1],
                        k_rows=k_rows,
                        v_rows=v_rows,
                        k_pos=k_pos,
                    ),
                    group_state,
                    group[1],
                    key_offset,
                )
                for group, group_state in zip(groups, states)
            )
        )

    finals = lax.fori_loop(0, row_count // block_rows, one_block, states)
    results = [(group_state[2], group_state[1]) for group_state in finals]
    rows_out = [
        (weighted / totals[:, :, None])
        .transpose(1, 0, 2)
        .reshape(weighted.shape[1], heads_att * HD)
        .astype(jnp.bfloat16)
        for weighted, totals in results
    ]
    attn_out = rows_out[0]
    return (mamba_out, attn_out)


def on_device(mixer_input, gate_input, b_proj, c_proj, decay_codes, *others):
    n = lax.axis_size("seq")
    rows, width = mixer_input.shape
    fits = (
        n == 2 * CHIPS
        and width == n * HD
        and decay_codes.shape[0] == 2 * n
        and b_proj.shape[1] == HD
        and rows == BLOCK
    )
    return (two_heads_each if fits else gathered)(
        mixer_input, gate_input, b_proj, c_proj, decay_codes, *others
    )


def solution(mesh):
    in_specs = (
        P("seq", "head"),
        P("seq", "head"),
        P("seq", None),
        P("seq", None),
        P("head", "seq"),
        P("head"),
        P("head"),
        P("head"),
        P("seq", "head"),
        P("seq", "head"),
    )
    out_specs = (P("seq", "head"), P("seq", "head"))
    return jax.shard_map(
        on_device, mesh=mesh, in_specs=in_specs, out_specs=out_specs, check_vma=False
    )
```

```python
import functools
import math

import jax
import jax.numpy as jnp
from jax import lax
from jax.experimental import pallas as pl
from jax.experimental.pallas import tpu as pltpu
from jax.sharding import PartitionSpec as P

HD = 128
CHANNELS_PER_HD = 64
BLOCK = 256


HIGH = lax.Precision.HIGHEST
NEG = -1e30
LOG2E = 1.4426950408889634
MIB = 1 << 20


VMEM = pl.BlockSpec(memory_space=pltpu.VMEM)
SMEM = pl.BlockSpec(memory_space=pltpu.SMEM)
HBM = pl.BlockSpec(memory_space=pltpu.HBM)
ANY = pl.BlockSpec(memory_space=pl.ANY)
CHIPS = 4
WIDE = 2 * HD
PARTS = 16


def call(body, outs, args, spaces, scratch=(), limit=16 * MIB):
    kinds = {"s": SMEM, "h": HBM, "a": ANY, "v": VMEM}
    spaces = spaces + "v" * (len(args) - len(spaces))
    return pl.pallas_call(
        body,
        out_shape=outs,
        in_specs=[kinds[space] for space in spaces],
        out_specs=jax.tree.map(lambda _: VMEM, outs),
        scratch_shapes=list(scratch),
        compiler_params=pltpu.CompilerParams(vmem_limit_bytes=limit),
        cost_estimate=pl.CostEstimate(flops=0, bytes_accessed=0, transcendentals=0),
    )(
        *(
            pltpu.with_memory_space_constraint(arg, pltpu.HBM) if space == "h" else arg
            for arg, space in zip(args, spaces)
        )
    )


def nt(a, b):
    return lax.dot_general(a, b, (((1,), (1,)), ((), ())), preferred_element_type=jnp.float32)


def nn(a, b):
    return jnp.dot(a, b, preferred_element_type=jnp.float32)


def step_counts(codes):
    rows = codes.shape[1]
    r = lax.broadcasted_iota(jnp.int32, (rows, rows), 0)
    s = lax.broadcasted_iota(jnp.int32, (rows, rows), 1)
    upper = (r <= s).astype(jnp.float32).astype(jnp.bfloat16)
    lower = (s <= r).astype(jnp.float32).astype(jnp.bfloat16)
    high = lax.shift_right_logical(codes, 7).astype(jnp.float32).astype(jnp.bfloat16)
    low = (codes & 127).astype(jnp.float32).astype(jnp.bfloat16)
    return (
        128.0 * nn(high, upper) + nn(low, upper),
        128.0 * nt(lower, high) + nt(lower, low),
    )


def left_lanes(rows):
    return lax.broadcasted_iota(jnp.int32, (rows, HD), 1) < CHANNELS_PER_HD


def chip_of(me):
    return lax.shift_right_logical(me, 1)


def around(chip, by):
    return (chip + by) & (CHIPS - 1)


def block_of(index, size):
    return pl.ds(pl.multiple_of(index * size, size), size)


def as_parts(total):
    total = jnp.broadcast_to(total, (PARTS, total.shape[1])).astype(jnp.int32)
    part = lax.broadcasted_iota(jnp.int32, total.shape, 0)
    high = lax.shift_right_logical(total, 16)
    middle = lax.shift_right_logical(total, 8) & 255
    chosen = jnp.where(
        part == 0, high, jnp.where(part == 1, middle, jnp.where(part == 2, total & 255, 0))
    )
    return chosen.astype(jnp.float32).astype(jnp.bfloat16)


def opened(rows):
    rows = rows.astype(jnp.float32)
    total = 65536.0 * rows[HD : HD + 1] + 256.0 * rows[HD + 1 : HD + 2] + rows[HD + 2 : HD + 3]
    return rows[:HD], total


def followed(first, second, slope):
    return jnp.exp2(second[1] * slope) * first[0] + second[0], first[1] + second[1]


def chunk_pairs(chip, steps, q_hbm, k_hbm, outs):
    rows = q_hbm.shape[0]
    pairs = []
    for d, out in zip(steps, outs):
        cols = block_of(around(chip, d), WIDE)
        pairs.append((q_hbm.at[:, cols], out.at[pl.ds(0, rows), :]))
        pairs.append((k_hbm.at[:, cols], out.at[pl.ds(rows, rows), :]))
    return pairs


def qk_kernel(me_ref, after_ref, q_hbm, k_hbm, *rest):
    pairs = chunk_pairs(chip_of(me_ref[0]), (1, 3), q_hbm, k_hbm, rest[:2])
    copies = [pltpu.make_async_copy(a, b, rest[2].at[i]) for i, (a, b) in enumerate(pairs)]
    for copy in copies:
        copy.start()
    for copy in copies:
        copy.wait()


def first_kernel(
    me_ref, rates_hbm, skip_hbm, codes_hbm, b_hbm, x_hbm, c_hbm, gate_hbm, gain_hbm, q_hbm, k_hbm,
    state_ref, slope_ref, skips_ref, codes_ref, b_ref, x_ref, c_ref, gate_ref, gain_ref, *rest
):
    qk, (rates_ref, skip_ref, sems) = rest[:2], rest[2:]
    rows = x_ref.shape[0]
    chip = chip_of(me_ref[0])
    pairs = [
        (codes_hbm, codes_ref),
        (b_hbm, b_ref),
        (rates_hbm, rates_ref),
        (x_hbm, x_ref),
        (skip_hbm, skip_ref),
        (c_hbm, c_ref),
        (gate_hbm, gate_ref),
        (gain_hbm, gain_ref),
    ]
    pairs += chunk_pairs(chip, (0, 2), q_hbm, k_hbm, qk)
    copies = [pltpu.make_async_copy(a, b, sems.at[i]) for i, (a, b) in enumerate(pairs)]
    for copy in copies:
        copy.start()
    copies[0].wait()
    _, counts = step_counts(codes_ref[...])
    copies[1].wait()
    b_turned = b_ref[...].astype(jnp.float32).T.astype(jnp.bfloat16)
    left = left_lanes(rows)
    copies[2].wait()
    copies[3].wait()
    for pair in range(x_ref.shape[1] // HD):
        cols = slice(pair * HD, (pair + 1) * HD)
        one, two = rates_ref[2 * pair], rates_ref[2 * pair + 1]
        slope_ref[:, cols] = jnp.where(left_lanes(8), one, two) * -LOG2E
        column = jnp.where(left, counts[:, 2 * pair : 2 * pair + 1], counts[:, 2 * pair + 1 : 2 * pair + 2])
        total = column[rows - 1 : rows, :]
        weight = jnp.exp2((total - column) * slope_ref[0:1, cols])
        x = (x_ref[:, cols].astype(jnp.float32) * weight).astype(jnp.bfloat16)
        state_ref[pl.ds(0, HD), cols] = nn(b_turned, x).astype(jnp.bfloat16)
        state_ref[pl.ds(HD, PARTS), cols] = as_parts(total)
    copies[4].wait()
    for pair in range(x_ref.shape[1] // HD):
        cols = slice(pair * HD, (pair + 1) * HD)
        skips_ref[:, cols] = jnp.where(left_lanes(8), skip_ref[2 * pair], skip_ref[2 * pair + 1])
    for copy in copies[5:]:
        copy.wait()


def chip_kernel(me_ref, slope_ref, own_ref, other_ref, out_ref):
    core = me_ref[0] & 1
    half = own_ref.shape[1] // 2
    cols = block_of(core, half)
    own, other = own_ref[:, cols], other_ref[:, cols]
    first = opened(jnp.where(core == 0, own, other))
    second = opened(jnp.where(core == 0, other, own))
    state, total = followed(first, second, slope_ref[0:1, cols])
    out_ref[pl.ds(0, HD), :] = state.astype(jnp.bfloat16)
    out_ref[pl.ds(HD, PARTS), :] = as_parts(total)


def two_chips_kernel(me_ref, after_ref, also_ref, slope_ref, own_ref, other_ref, out_ref):
    me = me_ref[0]
    odd = chip_of(me) & 1
    own, other = own_ref[...], other_ref[...]
    first = opened(jnp.where(odd == 0, own, other))
    second = opened(jnp.where(odd == 0, other, own))
    state, total = followed(first, second, slope_ref[0:1, block_of(me & 1, own.shape[1])])
    out_ref[pl.ds(0, HD), :] = state.astype(jnp.bfloat16)
    out_ref[pl.ds(HD, PARTS), :] = as_parts(total)


def ahead_kernel(me_ref, slope_ref, other_ref, far_ref, out_ref):
    me = me_ref[0]
    odd = chip_of(me) & 1
    near, total = opened(other_ref[...])
    near = jnp.where(odd == 1, near, 0.0)
    total = jnp.where(odd == 1, total, 0.0)
    far, _ = opened(far_ref[...])
    slope = slope_ref[0:1, block_of(me & 1, near.shape[1])]
    out_ref[...] = (jnp.exp2(total * slope) * far + near).astype(jnp.bfloat16)


def within_kernel(slope_ref, skips_ref, codes_ref, b_ref, x_ref, c_ref, gate_ref, own_ref, lead_ref):
    rows = x_ref.shape[0]
    across, down = step_counts(codes_ref[...])
    t = lax.broadcasted_iota(jnp.int32, (rows, rows), 0)
    s = lax.broadcasted_iota(jnp.int32, (rows, rows), 1)
    match = jnp.where(s <= t, nt(c_ref[...], b_ref[...]), 0.0)
    left = left_lanes(rows)
    for pair in range(x_ref.shape[1] // HD):
        cols = slice(pair * HD, (pair + 1) * HD)
        x = x_ref[:, cols]
        ys = []
        leads = []
        for h in (2 * pair, 2 * pair + 1):
            slope = slope_ref[0:1, h * CHANNELS_PER_HD : h * CHANNELS_PER_HD + 1]
            gap = jnp.maximum(down[:, h : h + 1] - across[h : h + 1, :], 0.0)
            ys.append(nn((jnp.exp2(gap * slope) * match).astype(jnp.bfloat16), x))
            leads.append(jnp.exp2(down[:, h : h + 1] * slope))
        gate = gate_ref[:, cols].astype(jnp.float32)
        gate = gate / (1.0 + jnp.exp(-gate))
        given = jnp.where(left, ys[0], ys[1]) + skips_ref[0:1, cols] * x.astype(jnp.float32)
        own_ref[:, cols] = given * gate
        lead_ref[:, cols] = jnp.where(left, leads[0], leads[1]) * gate


def gated_kernel(
    me_ref, slope_ref, local_ref, ahead_ref, other_ref, own_ref, lead_ref, c_ref, gated_ref, squares_ref
):
    core = me_ref[0] & 1
    c = c_ref[...]
    ones = jnp.ones((8, HD), jnp.bfloat16)
    squares = jnp.zeros(squares_ref.shape, jnp.float32)
    half = ahead_ref.shape[1]
    for at in range(0, 2 * half, HD):
        cols, within = slice(at, at + HD), slice(at % half, at % half + HD)
        state = jnp.where(core == at // half, ahead_ref[:, within], other_ref[:, within])
        state = state.astype(jnp.float32)
        later, _ = followed((state, 0.0), opened(local_ref[:, cols]), slope_ref[0:1, cols])
        state = jnp.where(core == 1, later, state).astype(jnp.bfloat16)
        gated = own_ref[:, cols] + lead_ref[:, cols] * nn(c, state)
        gated_ref[:, cols] = gated
        square = gated * gated
        high = square.astype(jnp.bfloat16)
        low = (square - high.astype(jnp.float32)).astype(jnp.bfloat16)
        squares = squares + nt(ones, high) + nt(ones, low)
    squares_ref[...] = squares


def turned(row):
    size = row.shape[1]
    r = lax.broadcasted_iota(jnp.int32, (size, size), 0)
    s = lax.broadcasted_iota(jnp.int32, (size, size), 1)
    return jnp.sum(jnp.where(r == s, jnp.broadcast_to(row, (size, size)), 0.0), axis=1, keepdims=True)


def norm_kernel(channels, me_ref, gain_ref, gated_ref, *rest):
    squares, out_ref, parts = rest[: -1 - CHIPS], rest[-1 - CHIPS], rest[-CHIPS:]
    chip = chip_of(me_ref[0])
    total = squares[0][0:1, :]
    for part in squares[1:]:
        total = total + part[0:1, :]
    column = turned(lax.rsqrt(total / channels + 1e-05))
    for d in range(CHIPS):
        cols = block_of(around(chip, d), WIDE)
        out = (gated_ref[:, cols] * column * gain_ref[:, cols]).astype(jnp.bfloat16)
        parts[d][...] = out
        out_ref[:, cols] = out


def keys_kernel(me_ref, after_ref, *rest):
    chip = chip_of(me_ref[0])
    rows = rest[0].shape[0] // 2
    for d in range(CHIPS):
        rest[CHIPS][block_of(around(chip, CHIPS - d), rows), :] = rest[d][pl.ds(rows, rows), :]


def weights_kernel(me_ref, own_ref, other_ref, *rest):
    ins, out_ref, q_ref = rest[:CHIPS], rest[CHIPS], rest[CHIPS + 1]
    rows = ins[0].shape[0] // 2
    me = me_ref[0]
    chip, core = chip_of(me), me & 1
    for d in range(CHIPS):
        q_ref[block_of(around(chip, CHIPS - d), rows), :] = ins[d][pl.ds(0, rows), :]
    scale = LOG2E / math.sqrt(HD)
    half = rows // 2
    for head in range(2):
        lanes = slice(head * HD, (head + 1) * HD)
        for i in range(2 * CHIPS):
            seen = (i // 2) * rows
            q = q_ref[pl.ds(i * half, half), lanes]
            t = lax.broadcasted_iota(jnp.int32, (half, rows), 0) + (i % 2) * half
            s = lax.broadcasted_iota(jnp.int32, (half, rows), 1)
            blocks = []
            for keys_ref, base, shown in (
                (own_ref, 0, s <= t),
                (other_ref, CHIPS * rows, s < core * rows),
            ):
                for at in range(0, seen, rows):
                    blocks.append((base + at, nt(q, keys_ref[pl.ds(at, rows), lanes])))
                last = nt(q, keys_ref[pl.ds(seen, rows), lanes])
                blocks.append((base + seen, jnp.where(shown, last, NEG)))
            top = functools.reduce(jnp.maximum, [block for _, block in blocks])
            top = jnp.max(top, axis=1, keepdims=True) * scale
            blocks = [(at, jnp.exp2(block * scale - top)) for at, block in blocks]
            total = functools.reduce(jnp.add, [block for _, block in blocks])
            inverse = 1.0 / jnp.sum(total, axis=1, keepdims=True)
            for at, block in blocks:
                out_ref[head, pl.ds(i * half, half), pl.ds(at, rows)] = (block * inverse).astype(
                    jnp.bfloat16
                )


def passed_kernel(after_ref, in_ref, out_ref):
    out_ref[...] = in_ref[...]


def weighted(weights_ref, head, i, rows, base, v_ref):
    seen = (i + 1) * rows
    lanes = slice(head * HD, (head + 1) * HD)
    held = weights_ref[head, pl.ds(i * rows, rows), pl.ds(base, seen)]
    return nn(held, v_ref[pl.ds(0, seen), lanes])


def in_place(me_ref, parts, v_ref):
    chip = chip_of(me_ref[0])
    for d, part in enumerate(parts):
        v_ref[block_of(around(chip, CHIPS - d), part.shape[0]), :] = part[...]


def own_values_kernel(me_ref, weights_ref, *rest):
    own, out_ref, v_ref = rest[:CHIPS], rest[CHIPS], rest[CHIPS + 1]
    rows = own[0].shape[0]
    in_place(me_ref, own, v_ref)
    for i in range(CHIPS):
        for head in range(2):
            lanes = slice(head * HD, (head + 1) * HD)
            out_ref[pl.ds(i * rows, rows), lanes] = weighted(weights_ref, head, i, rows, 0, v_ref)


def values_kernel(me_ref, partial_ref, weights_ref, *rest):
    other, outs, v_ref, o_ref = rest[:CHIPS], rest[CHIPS : 2 * CHIPS], *rest[2 * CHIPS :]
    rows = other[0].shape[0]
    in_place(me_ref, other, v_ref)
    for i in range(CHIPS):
        for head in range(2):
            at, lanes = pl.ds(i * rows, rows), slice(head * HD, (head + 1) * HD)
            more = weighted(weights_ref, head, i, rows, CHIPS * rows, v_ref)
            o_ref[at, lanes] = (partial_ref[at, lanes] + more).astype(jnp.bfloat16)
    chip = chip_of(me_ref[0])
    for d in range(CHIPS):
        outs[d][...] = o_ref[block_of(around(chip, d), rows), :]


def join_kernel(me_ref, *rest):
    chip = chip_of(me_ref[0])
    for d in range(CHIPS):
        rest[CHIPS][:, block_of(around(chip, CHIPS - d), WIDE)] = rest[d][...]


def shifted(part, d):
    n = 2 * CHIPS
    return lax.ppermute(part, "seq", [(i, (i + 2 * d) % n) for i in range(n)])


def exchange(parts):
    return [parts[0]] + [shifted(parts[d], d) for d in range(1, CHIPS)]


def swapped(part):
    return lax.ppermute(part, "seq", [(i, i ^ 1) for i in range(2 * CHIPS)])


def two_heads_each(
    mixer_input,
    gate_input,
    b_proj,
    c_proj,
    decay_codes,
    decay_rates,
    skip_gain,
    norm_gain,
    queries,
    keys,
):
    n, m = lax.axis_size("seq"), lax.axis_size("head")
    rows, width = mixer_input.shape
    heads = decay_codes.shape[0]
    me = lax.axis_index("seq").astype(jnp.int32).reshape(1)
    shape = pltpu.VMEM
    bf16, f32 = jnp.bfloat16, jnp.float32
    chunk = shape((rows, WIDE), bf16)
    half_state = shape((HD + PARTS, width // 2), bf16)

    state, slope, skips, codes, b, x, c, gate, gain, qk_own, qk_two = call(
        first_kernel,
        [shape((HD + PARTS, width), bf16), shape((8, width), f32), shape((8, width), f32)]
        + [
            shape(decay_codes.shape, jnp.int32),
            shape(b_proj.shape, bf16),
            shape((rows, width), bf16),
            shape(c_proj.shape, bf16),
            shape((rows, width), bf16),
            shape((1, width), f32),
        ]
        + [shape((2 * rows, WIDE), bf16)] * 2,
        (me, decay_rates, skip_gain, decay_codes, b_proj, mixer_input, c_proj)
        + (gate_input, norm_gain.reshape(1, width), queries, keys),
        "shhhhhhhhhh",
        [
            pltpu.SMEM((heads,), f32),
            pltpu.SMEM((heads,), f32),
            pltpu.SemaphoreType.DMA((12,)),
        ],
    )
    other = swapped(state)
    qk_two = shifted(qk_two, 2)
    own, lead = call(
        within_kernel,
        [shape((rows, width), f32)] * 2,
        (slope, skips, codes, b, x, c, gate),
        "",
    )
    chip_state = call(chip_kernel, half_state, (me, slope, state, other), "s")
    chip_other = lax.ppermute(chip_state, "seq", [(i, i ^ 2) for i in range(n)])
    two_chips = call(
        two_chips_kernel, half_state, (me, own, qk_two, slope, chip_state, chip_other), "saa"
    )
    far = lax.ppermute(two_chips, "seq", [(i, i + 4) for i in range(n // 2)])
    qk_one, qk_three = call(
        qk_kernel,
        [shape((2 * rows, WIDE), bf16)] * 2,
        (me, far, queries, keys),
        "sahh",
        [pltpu.SemaphoreType.DMA((4,))],
    )
    qk = [qk_own, shifted(qk_one, 1), qk_two, shifted(qk_three, 3)]
    ahead = call(
        ahead_kernel, shape((HD, width // 2), bf16), (me, slope, chip_other, far), "s"
    )
    gated, squares = call(
        gated_kernel,
        [shape((rows, width), f32), shape((8, rows), f32)],
        (me, slope, other, ahead, swapped(ahead), own, lead, c),
        "s",
    )
    squares = [squares] + [
        lax.ppermute(squares, "head", [(i, (i + k) % m) for i in range(m)]) for k in range(1, m)
    ]
    mamba_out, *values = call(
        functools.partial(norm_kernel, width * m),
        [jax.ShapeDtypeStruct((rows, width), bf16)] + [chunk] * CHIPS,
        (me, gain, gated, *squares),
        "s",
    )
    values = exchange(values)
    own_keys = call(
        keys_kernel,
        shape((CHIPS * rows, WIDE), bf16),
        (me, values[0], *qk),
        "sa",
    )
    weights = call(
        weights_kernel,
        shape((2, CHIPS * rows, n * rows), bf16),
        (me, own_keys, swapped(own_keys), *qk),
        "s",
        [pltpu.VMEM((CHIPS * rows, WIDE), bf16)],
        limit=24 * MIB,
    )
    passed = [call(passed_kernel, chunk, (weights, part), "a") for part in values[1:]]
    other_values = [swapped(part) for part in (values[0], *passed)]
    partial_sums = call(
        own_values_kernel,
        shape((CHIPS * rows, WIDE), f32),
        (me, weights, *values),
        "s",
        [pltpu.VMEM((CHIPS * rows, WIDE), bf16)],
    )
    results = call(
        values_kernel,
        [chunk] * CHIPS,
        (me, partial_sums, weights, *other_values),
        "s",
        [pltpu.VMEM((CHIPS * rows, WIDE), bf16), pltpu.VMEM((CHIPS * rows, WIDE), bf16)],
    )
    attn_out = call(
        join_kernel,
        jax.ShapeDtypeStruct((rows, width), bf16),
        (me, *exchange(results)),
        "s",
    )
    return (mamba_out, attn_out)


def running_sum(log_decay):
    span = log_decay.shape[1]
    at = jnp.arange(span, dtype=jnp.int32)
    earlier = (at[:, None] <= at[None, :]).astype(jnp.float32)
    return jnp.dot(log_decay, earlier, precision=HIGH)


def carried_in(array, axis, combine, identity):
    devices, mine = (lax.axis_size(axis), lax.axis_index(axis))
    everything = jax.tree.map(
        lambda part, kind: lax.all_gather(part.astype(kind), axis),
        array,
        (jnp.bfloat16, jnp.bfloat16),
    )
    start = jax.tree.map(
        lambda part, zero: jnp.broadcast_to(jnp.asarray(zero, part.dtype), part.shape),
        array,
        identity,
    )

    def hop(k, before):
        reached = k < mine
        new = combine(
            before, jax.tree.map(lambda part, own: part[k].astype(own.dtype), everything, array)
        )
        return jax.tree.map(lambda a, b: jnp.where(reached, a, b), new, before)

    return lax.fori_loop(0, devices, hop, start)


def block_step(state_carry, inputs):
    x_block, b_block, c_block, decay_block = inputs
    running = running_sum(decay_block)
    span = decay_block.shape[1]
    causal = (
        jnp.arange(span, dtype=jnp.int32)[:, None] >= jnp.arange(span, dtype=jnp.int32)[None, :]
    )
    log_gaps = jnp.where(causal[None, :, :], running[:, :, None] - running[:, None, :], NEG)
    decays = jnp.exp(log_gaps)
    match_strength = jnp.dot(c_block, b_block.T, preferred_element_type=jnp.float32)
    x_float = x_block.astype(jnp.float32)
    within = jnp.einsum(
        "hts,shp->thp", decays * match_strength[None, :, :], x_float, precision=HIGH
    )
    c_float = c_block.astype(jnp.float32)
    carried = jnp.exp(running).T[:, :, None] * jnp.einsum(
        "tn,hnp->thp", c_float, state_carry, precision=HIGH
    )
    to_end = jnp.exp(running[:, -1:] - running)
    updated_state = jnp.exp(running[:, -1])[:, None, None] * state_carry + jnp.einsum(
        "hs,sn,shp->hnp", to_end, b_block.astype(jnp.float32), x_float, precision=HIGH
    )
    return (updated_state, within + carried)


def local_scan(x_local, b_local, c_local, log_decay):
    tok_rows = x_local.shape[0]
    heads_local = log_decay.shape[0]
    block_count = tok_rows // BLOCK
    x_blocks = x_local.reshape(block_count, BLOCK, heads_local, CHANNELS_PER_HD)
    b_blocks = b_local.reshape(block_count, BLOCK, b_local.shape[1])
    c_blocks = c_local.reshape(block_count, BLOCK, c_local.shape[1])
    decay_blocks = log_decay.reshape(heads_local, block_count, BLOCK).transpose(1, 0, 2)
    initial = jnp.zeros((heads_local, b_local.shape[1], CHANNELS_PER_HD), jnp.float32)
    final_state, y_blocks = lax.scan(
        block_step, initial, (x_blocks, b_blocks, c_blocks, decay_blocks)
    )
    return (final_state, y_blocks.reshape(tok_rows, heads_local, CHANNELS_PER_HD))


def masked_scores(q_rows, q_pos, k_rows, k_pos):
    score_scale = 1.0 / math.sqrt(k_rows.shape[-1])
    scores = (
        jnp.einsum("qhd,khd->hqk", q_rows, k_rows, preferred_element_type=jnp.float32) * score_scale
    )
    visible = k_pos[None, None, :] <= q_pos[None, :, None]
    return (jnp.where(visible, scores, NEG), visible)


def online_update(group_state, q_rows, q_pos, k_rows, v_rows, k_pos):
    row_top, row_total, weighted_sum = group_state
    scores, visible = masked_scores(q_rows, q_pos, k_rows, k_pos)
    new_top = jnp.maximum(row_top, jnp.max(scores, axis=2))
    rescale = jnp.exp(row_top - new_top)
    weights = jnp.where(visible, jnp.exp(scores - new_top[:, :, None]), 0.0)
    row_total = row_total * rescale + jnp.sum(weights, axis=2)
    weighted_sum = weighted_sum * rescale[:, :, None] + jnp.einsum(
        "hqk,khd->hqd", weights.astype(jnp.bfloat16), v_rows, preferred_element_type=jnp.float32
    )
    return (new_top, row_total, weighted_sum)


def when_visible(state_update, group_state, q_pos, key_offset):
    return lax.cond(key_offset > q_pos[-1], lambda held: held, state_update, group_state)


def gathered(
    mixer_input,
    gate_input,
    b_proj,
    c_proj,
    decay_codes,
    decay_rates,
    skip_gain,
    norm_gain,
    queries,
    keys,
):
    tok_rows = mixer_input.shape[0]
    heads_local = decay_rates.shape[0]
    heads_att = queries.shape[1] // HD
    seq_rank = lax.axis_index("seq")
    own_positions = seq_rank * tok_rows + jnp.arange(tok_rows, dtype=jnp.int32)
    groups = [(queries, own_positions)]
    groups = [(q_rows.reshape(q_rows.shape[0], heads_att, HD), q_pos) for q_rows, q_pos in groups]
    log_decay = -decay_rates[:, None] * decay_codes.astype(jnp.float32)
    local_state, y_local = local_scan(mixer_input, b_proj, c_proj, log_decay)
    total_log = jnp.sum(log_decay, axis=1)

    def combine(earlier, later):
        return (earlier[0] + later[0], jnp.exp(later[0])[:, None, None] * earlier[1] + later[1])

    identity = (jnp.zeros_like(total_log), jnp.zeros_like(local_state))
    _, incoming = carried_in((total_log, local_state), "seq", combine, identity)
    running = running_sum(log_decay)
    carried = jnp.einsum("tn,hnp->thp", c_proj.astype(jnp.float32), incoming, precision=HIGH)
    carried = carried * jnp.exp(running).T[:, :, None]
    x_float = mixer_input.reshape(tok_rows, heads_local, CHANNELS_PER_HD).astype(jnp.float32)
    ssm_out = (y_local + carried + skip_gain[None, :, None] * x_float).reshape(
        tok_rows, heads_local * CHANNELS_PER_HD
    )
    gated = ssm_out * jax.nn.silu(gate_input.astype(jnp.float32))
    squares = lax.psum(jnp.sum(gated * gated, axis=1), "head")
    channels = gated.shape[1] * lax.axis_size("head")
    mamba_out = (
        gated * lax.rsqrt(squares / channels + 1e-05)[:, None] * norm_gain[None, :]
    ).astype(jnp.bfloat16)
    initial = tuple(
        (
            (
                jnp.full((heads_att, q_pos.shape[0]), NEG, jnp.float32),
                jnp.zeros((heads_att, q_pos.shape[0]), jnp.float32),
                jnp.zeros((heads_att, q_pos.shape[0], HD), jnp.float32),
            )
            for _, q_pos in groups
        )
    )
    states = initial
    k_piece = lax.all_gather(keys, "seq", axis=0, tiled=True)
    v_piece = lax.all_gather(mamba_out, "seq", axis=0, tiled=True)
    row_count = k_piece.shape[0]
    block_rows = math.gcd(row_count, 512)

    def one_block(block_id, states):
        key_offset = block_id * block_rows
        k_rows = lax.dynamic_slice_in_dim(k_piece, block_id * block_rows, block_rows, 0).reshape(
            block_rows, heads_att, HD
        )
        v_rows = lax.dynamic_slice_in_dim(v_piece, block_id * block_rows, block_rows, 0).reshape(
            block_rows, heads_att, HD
        )
        k_pos = key_offset + jnp.arange(block_rows, dtype=jnp.int32)
        return tuple(
            (
                when_visible(
                    functools.partial(
                        online_update,
                        q_rows=group[0],
                        q_pos=group[1],
                        k_rows=k_rows,
                        v_rows=v_rows,
                        k_pos=k_pos,
                    ),
                    group_state,
                    group[1],
                    key_offset,
                )
                for group, group_state in zip(groups, states)
            )
        )

    finals = lax.fori_loop(0, row_count // block_rows, one_block, states)
    results = [(group_state[2], group_state[1]) for group_state in finals]
    rows_out = [
        (weighted / totals[:, :, None])
        .transpose(1, 0, 2)
        .reshape(weighted.shape[1], heads_att * HD)
        .astype(jnp.bfloat16)
        for weighted, totals in results
    ]
    attn_out = rows_out[0]
    return (mamba_out, attn_out)


def on_device(mixer_input, gate_input, b_proj, c_proj, decay_codes, *others):
    n = lax.axis_size("seq")
    rows, width = mixer_input.shape
    fits = (
        n == 2 * CHIPS
        and width == n * HD
        and decay_codes.shape[0] == 2 * n
        and b_proj.shape[1] == HD
        and rows == BLOCK
    )
    return (two_heads_each if fits else gathered)(
        mixer_input, gate_input, b_proj, c_proj, decay_codes, *others
    )


def solution(mesh):
    in_specs = (
        P("seq", "head"),
        P("seq", "head"),
        P("seq", None),
        P("seq", None),
        P("head", "seq"),
        P("head"),
        P("head"),
        P("head"),
        P("seq", "head"),
        P("seq", "head"),
    )
    out_specs = (P("seq", "head"), P("seq", "head"))
    return jax.shard_map(
        on_device, mesh=mesh, in_specs=in_specs, out_specs=out_specs, check_vma=False
    )
```

```python
import functools
import math

import jax
import jax.numpy as jnp
from jax import lax
from jax.experimental import pallas as pl
from jax.experimental.pallas import tpu as pltpu
from jax.sharding import PartitionSpec as P

HD = 128
CHANNELS_PER_HD = 64
BLOCK = 256


HIGH = lax.Precision.HIGHEST
NEG = -1e30
LOG2E = 1.4426950408889634
MIB = 1 << 20


VMEM = pl.BlockSpec(memory_space=pltpu.VMEM)
SMEM = pl.BlockSpec(memory_space=pltpu.SMEM)
HBM = pl.BlockSpec(memory_space=pltpu.HBM)
ANY = pl.BlockSpec(memory_space=pl.ANY)
CHIPS = 4
WIDE = 2 * HD
PARTS = 16


def call(body, outs, args, spaces, scratch=(), limit=16 * MIB, through=0):
    kinds = {"s": SMEM, "h": HBM, "a": ANY, "v": VMEM}
    spaces = spaces + "v" * (len(args) - len(spaces))
    return pl.pallas_call(
        body,
        out_shape=outs,
        in_specs=[kinds[space] for space in spaces],
        out_specs=[ANY if i >= len(outs) - through else VMEM for i in range(len(outs))]
        if through
        else jax.tree.map(lambda _: VMEM, outs),
        input_output_aliases={len(args) - i: len(outs) - i for i in range(1, through + 1)},
        scratch_shapes=list(scratch),
        compiler_params=pltpu.CompilerParams(vmem_limit_bytes=limit),
        cost_estimate=pl.CostEstimate(flops=0, bytes_accessed=0, transcendentals=0),
    )(
        *(
            pltpu.with_memory_space_constraint(arg, pltpu.HBM) if space == "h" else arg
            for arg, space in zip(args, spaces)
        )
    )


def nt(a, b):
    return lax.dot_general(a, b, (((1,), (1,)), ((), ())), preferred_element_type=jnp.float32)


def nn(a, b):
    return jnp.dot(a, b, preferred_element_type=jnp.float32)


def step_counts(codes):
    rows = codes.shape[1]
    r = lax.broadcasted_iota(jnp.int32, (rows, rows), 0)
    s = lax.broadcasted_iota(jnp.int32, (rows, rows), 1)
    upper = (r <= s).astype(jnp.float32).astype(jnp.bfloat16)
    lower = (s <= r).astype(jnp.float32).astype(jnp.bfloat16)
    high = lax.shift_right_logical(codes, 7).astype(jnp.float32).astype(jnp.bfloat16)
    low = (codes & 127).astype(jnp.float32).astype(jnp.bfloat16)
    return (
        128.0 * nn(high, upper) + nn(low, upper),
        128.0 * nt(lower, high) + nt(lower, low),
    )


def left_lanes(rows):
    return lax.broadcasted_iota(jnp.int32, (rows, HD), 1) < CHANNELS_PER_HD


def chip_of(me):
    return lax.shift_right_logical(me, 1)


def across(chip, by):
    return chip ^ by


def block_of(index, size):
    return pl.ds(pl.multiple_of(index * size, size), size)


def as_parts(total):
    total = jnp.broadcast_to(total, (PARTS, total.shape[1])).astype(jnp.int32)
    part = lax.broadcasted_iota(jnp.int32, total.shape, 0)
    high = lax.shift_right_logical(total, 16)
    middle = lax.shift_right_logical(total, 8) & 255
    chosen = jnp.where(
        part == 0, high, jnp.where(part == 1, middle, jnp.where(part == 2, total & 255, 0))
    )
    return chosen.astype(jnp.float32).astype(jnp.bfloat16)


def opened(rows):
    rows = rows.astype(jnp.float32)
    total = 65536.0 * rows[HD : HD + 1] + 256.0 * rows[HD + 1 : HD + 2] + rows[HD + 2 : HD + 3]
    return rows[:HD], total


def followed(first, second, slope):
    return jnp.exp2(second[1] * slope) * first[0] + second[0], first[1] + second[1]


def chunk_pairs(chip, steps, q_hbm, k_hbm, outs):
    rows = q_hbm.shape[0]
    pairs = []
    for d, out in zip(steps, outs):
        cols = block_of(across(chip, d), WIDE)
        pairs.append((q_hbm.at[:, cols], out.at[pl.ds(0, rows), :]))
        pairs.append((k_hbm.at[:, cols], out.at[pl.ds(rows, rows), :]))
    return pairs


def first_kernel(
    me_ref, rates_hbm, skip_hbm, codes_hbm, b_hbm, x_hbm, c_hbm, gate_hbm, gain_hbm, q_hbm, k_hbm,
    state_ref, slope_ref, skips_ref, codes_ref, b_ref, x_ref, c_ref, gate_ref, gain_ref, *rest
):
    qk, (rates_ref, skip_ref, sems) = rest[:CHIPS], rest[CHIPS:]
    rows = x_ref.shape[0]
    chip = chip_of(me_ref[0])
    pairs = [
        (codes_hbm, codes_ref),
        (b_hbm, b_ref),
        (rates_hbm, rates_ref),
        (x_hbm, x_ref),
        (skip_hbm, skip_ref),
        (c_hbm, c_ref),
        (gate_hbm, gate_ref),
        (gain_hbm, gain_ref),
    ]
    pairs += chunk_pairs(chip, (0, 1, 2, 3), q_hbm, k_hbm, qk)
    copies = [pltpu.make_async_copy(a, b, sems.at[i]) for i, (a, b) in enumerate(pairs)]
    for copy in copies:
        copy.start()
    copies[0].wait()
    _, counts = step_counts(codes_ref[...])
    copies[1].wait()
    b_turned = b_ref[...].astype(jnp.float32).T.astype(jnp.bfloat16)
    left = left_lanes(rows)
    copies[2].wait()
    copies[3].wait()
    for pair in range(x_ref.shape[1] // HD):
        cols = slice(pair * HD, (pair + 1) * HD)
        one, two = rates_ref[2 * pair], rates_ref[2 * pair + 1]
        slope_ref[:, cols] = jnp.where(left_lanes(8), one, two) * -LOG2E
        column = jnp.where(left, counts[:, 2 * pair : 2 * pair + 1], counts[:, 2 * pair + 1 : 2 * pair + 2])
        total = column[rows - 1 : rows, :]
        weight = jnp.exp2((total - column) * slope_ref[0:1, cols])
        x = (x_ref[:, cols].astype(jnp.float32) * weight).astype(jnp.bfloat16)
        state_ref[pl.ds(0, HD), cols] = nn(b_turned, x).astype(jnp.bfloat16)
        state_ref[pl.ds(HD, PARTS), cols] = as_parts(total)
    copies[4].wait()
    for pair in range(x_ref.shape[1] // HD):
        cols = slice(pair * HD, (pair + 1) * HD)
        skips_ref[:, cols] = jnp.where(left_lanes(8), skip_ref[2 * pair], skip_ref[2 * pair + 1])
    for copy in copies[5:]:
        copy.wait()


def chip_kernel(me_ref, slope_ref, own_ref, other_ref, out_ref):
    core = me_ref[0] & 1
    half = own_ref.shape[1] // 2
    cols = block_of(core, half)
    own, other = own_ref[:, cols], other_ref[:, cols]
    first = opened(jnp.where(core == 0, own, other))
    second = opened(jnp.where(core == 0, other, own))
    state, total = followed(first, second, slope_ref[0:1, cols])
    out_ref[pl.ds(0, HD), :] = state.astype(jnp.bfloat16)
    out_ref[pl.ds(HD, PARTS), :] = as_parts(total)


def two_chips_kernel(me_ref, after_ref, slope_ref, own_ref, other_ref, *rest):
    out_ref = rest[1]
    me = me_ref[0]
    odd = chip_of(me) & 1
    own, other = own_ref[...], other_ref[...]
    first = opened(jnp.where(odd == 0, own, other))
    second = opened(jnp.where(odd == 0, other, own))
    state, total = followed(first, second, slope_ref[0:1, block_of(me & 1, own.shape[1])])
    out_ref[pl.ds(0, HD), :] = state.astype(jnp.bfloat16)
    out_ref[pl.ds(HD, PARTS), :] = as_parts(total)


def ahead_kernel(me_ref, after_ref, slope_ref, other_ref, far_ref, *rest):
    me = me_ref[0]
    odd = chip_of(me) & 1
    near, total = opened(other_ref[...])
    near = jnp.where(odd == 1, near, 0.0)
    total = jnp.where(odd == 1, total, 0.0)
    far, _ = opened(far_ref[...])
    slope = slope_ref[0:1, block_of(me & 1, near.shape[1])]
    rest[1][...] = (jnp.exp2(total * slope) * far + near).astype(jnp.bfloat16)


def within_kernel(slope_ref, skips_ref, codes_ref, b_ref, x_ref, c_ref, gate_ref, own_ref, lead_ref):
    rows = x_ref.shape[0]
    across, down = step_counts(codes_ref[...])
    t = lax.broadcasted_iota(jnp.int32, (rows, rows), 0)
    s = lax.broadcasted_iota(jnp.int32, (rows, rows), 1)
    match = jnp.where(s <= t, nt(c_ref[...], b_ref[...]), 0.0)
    left = left_lanes(rows)
    for pair in range(x_ref.shape[1] // HD):
        cols = slice(pair * HD, (pair + 1) * HD)
        x = x_ref[:, cols]
        ys = []
        leads = []
        for h in (2 * pair, 2 * pair + 1):
            slope = slope_ref[0:1, h * CHANNELS_PER_HD : h * CHANNELS_PER_HD + 1]
            gap = jnp.maximum(down[:, h : h + 1] - across[h : h + 1, :], 0.0)
            ys.append(nn((jnp.exp2(gap * slope) * match).astype(jnp.bfloat16), x))
            leads.append(jnp.exp2(down[:, h : h + 1] * slope))
        gate = gate_ref[:, cols].astype(jnp.float32)
        gate = gate / (1.0 + jnp.exp(-gate))
        given = jnp.where(left, ys[0], ys[1]) + skips_ref[0:1, cols] * x.astype(jnp.float32)
        own_ref[:, cols] = given * gate
        lead_ref[:, cols] = jnp.where(left, leads[0], leads[1]) * gate


def gated_kernel(
    me_ref, slope_ref, local_ref, ahead_ref, other_ref, own_ref, lead_ref, c_ref, gated_ref, squares_ref
):
    core = me_ref[0] & 1
    c = c_ref[...]
    ones = jnp.ones((8, HD), jnp.bfloat16)
    squares = jnp.zeros(squares_ref.shape, jnp.float32)
    half = ahead_ref.shape[1]
    for at in range(0, 2 * half, HD):
        cols, within = slice(at, at + HD), slice(at % half, at % half + HD)
        state = jnp.where(core == at // half, ahead_ref[:, within], other_ref[:, within])
        state = state.astype(jnp.float32)
        later, _ = followed((state, 0.0), opened(local_ref[:, cols]), slope_ref[0:1, cols])
        state = jnp.where(core == 1, later, state).astype(jnp.bfloat16)
        gated = own_ref[:, cols] + lead_ref[:, cols] * nn(c, state)
        gated_ref[:, cols] = gated
        square = gated * gated
        high = square.astype(jnp.bfloat16)
        low = (square - high.astype(jnp.float32)).astype(jnp.bfloat16)
        squares = squares + nt(ones, high) + nt(ones, low)
    squares_ref[...] = squares


def turned(row):
    size = row.shape[1]
    r = lax.broadcasted_iota(jnp.int32, (size, size), 0)
    s = lax.broadcasted_iota(jnp.int32, (size, size), 1)
    return jnp.sum(jnp.where(r == s, jnp.broadcast_to(row, (size, size)), 0.0), axis=1, keepdims=True)


def norm_kernel(channels, me_ref, gain_ref, gated_ref, *rest):
    squares, out_ref, parts = rest[: -1 - CHIPS], rest[-1 - CHIPS], rest[-CHIPS:]
    chip = chip_of(me_ref[0])
    total = squares[0][0:1, :]
    for part in squares[1:]:
        total = total + part[0:1, :]
    column = turned(lax.rsqrt(total / channels + 1e-05))
    for d in range(CHIPS):
        cols = block_of(across(chip, d), WIDE)
        out = (gated_ref[:, cols] * column * gain_ref[:, cols]).astype(jnp.bfloat16)
        parts[d][...] = out
        out_ref[:, cols] = out


def keys_kernel(me_ref, after_ref, *rest):
    chip = chip_of(me_ref[0])
    rows = rest[0].shape[0] // 2
    for d in range(CHIPS):
        rest[CHIPS][block_of(across(chip, d), rows), :] = rest[d][pl.ds(rows, rows), :]


def weights_kernel(me_ref, own_ref, other_ref, *rest):
    ins, out_ref, q_ref = rest[:CHIPS], rest[CHIPS], rest[CHIPS + 1]
    rows = ins[0].shape[0] // 2
    me = me_ref[0]
    chip, core = chip_of(me), me & 1
    for d in range(CHIPS):
        q_ref[block_of(across(chip, d), rows), :] = ins[d][pl.ds(0, rows), :]
    scale = LOG2E / math.sqrt(HD)
    half = rows // 2
    for head in range(2):
        lanes = slice(head * HD, (head + 1) * HD)
        for i in range(2 * CHIPS):
            seen = (i // 2) * rows
            q = q_ref[pl.ds(i * half, half), lanes]
            t = lax.broadcasted_iota(jnp.int32, (half, rows), 0) + (i % 2) * half
            s = lax.broadcasted_iota(jnp.int32, (half, rows), 1)
            blocks = []
            for keys_ref, base, shown in (
                (own_ref, 0, s <= t),
                (other_ref, CHIPS * rows, s < core * rows),
            ):
                for at in range(0, seen, rows):
                    blocks.append((base + at, nt(q, keys_ref[pl.ds(at, rows), lanes])))
                last = nt(q, keys_ref[pl.ds(seen, rows), lanes])
                blocks.append((base + seen, jnp.where(shown, last, NEG)))
            top = functools.reduce(jnp.maximum, [block for _, block in blocks])
            top = jnp.max(top, axis=1, keepdims=True) * scale
            blocks = [(at, jnp.exp2(block * scale - top)) for at, block in blocks]
            total = functools.reduce(jnp.add, [block for _, block in blocks])
            inverse = 1.0 / jnp.sum(total, axis=1, keepdims=True)
            for at, block in blocks:
                out_ref[head, pl.ds(i * half, half), pl.ds(at, rows)] = (block * inverse).astype(
                    jnp.bfloat16
                )


def passed_kernel(after_ref, in_ref, out_ref):
    out_ref[...] = in_ref[...]


def weighted(weights_ref, head, i, rows, base, v_ref):
    seen = (i + 1) * rows
    lanes = slice(head * HD, (head + 1) * HD)
    held = weights_ref[head, pl.ds(i * rows, rows), pl.ds(base, seen)]
    return nn(held, v_ref[pl.ds(0, seen), lanes])


def in_place(me_ref, parts, v_ref):
    chip = chip_of(me_ref[0])
    for d, part in enumerate(parts):
        v_ref[block_of(across(chip, d), part.shape[0]), :] = part[...]


def own_values_kernel(me_ref, weights_ref, *rest):
    own, out_ref, v_ref = rest[:CHIPS], rest[CHIPS], rest[CHIPS + 1]
    rows = own[0].shape[0]
    in_place(me_ref, own, v_ref)
    for i in range(CHIPS):
        for head in range(2):
            lanes = slice(head * HD, (head + 1) * HD)
            out_ref[pl.ds(i * rows, rows), lanes] = weighted(weights_ref, head, i, rows, 0, v_ref)


def values_kernel(me_ref, partial_ref, weights_ref, *rest):
    other, outs, v_ref, o_ref = rest[:CHIPS], rest[CHIPS : 2 * CHIPS], *rest[2 * CHIPS :]
    rows = other[0].shape[0]
    in_place(me_ref, other, v_ref)
    for i in range(CHIPS):
        for head in range(2):
            at, lanes = pl.ds(i * rows, rows), slice(head * HD, (head + 1) * HD)
            more = weighted(weights_ref, head, i, rows, CHIPS * rows, v_ref)
            o_ref[at, lanes] = (partial_ref[at, lanes] + more).astype(jnp.bfloat16)
    chip = chip_of(me_ref[0])
    for d in range(CHIPS):
        outs[d][...] = o_ref[block_of(across(chip, d), rows), :]


def join_kernel(me_ref, *rest):
    chip = chip_of(me_ref[0])
    for d in range(CHIPS):
        rest[CHIPS][:, block_of(across(chip, d), WIDE)] = rest[d][...]


def shifted(part, d):
    return lax.ppermute(part, "seq", [(i, i ^ (2 * d)) for i in range(2 * CHIPS)])


def exchange(parts):
    return [parts[0]] + [shifted(parts[d], d) for d in range(1, CHIPS)]


def swapped(part):
    return lax.ppermute(part, "seq", [(i, i ^ 1) for i in range(2 * CHIPS)])


def two_heads_each(
    mixer_input,
    gate_input,
    b_proj,
    c_proj,
    decay_codes,
    decay_rates,
    skip_gain,
    norm_gain,
    queries,
    keys,
):
    n, m = lax.axis_size("seq"), lax.axis_size("head")
    rows, width = mixer_input.shape
    heads = decay_codes.shape[0]
    me = lax.axis_index("seq").astype(jnp.int32).reshape(1)
    shape = pltpu.VMEM
    bf16, f32 = jnp.bfloat16, jnp.float32
    chunk = shape((rows, WIDE), bf16)
    half_state = shape((HD + PARTS, width // 2), bf16)

    state, slope, skips, codes, b, x, c, gate, gain, qk_own, qk_one, qk_two, qk_three = call(
        first_kernel,
        [shape((HD + PARTS, width), bf16), shape((8, width), f32), shape((8, width), f32)]
        + [
            shape(decay_codes.shape, jnp.int32),
            shape(b_proj.shape, bf16),
            shape((rows, width), bf16),
            shape(c_proj.shape, bf16),
            shape((rows, width), bf16),
            shape((1, width), f32),
        ]
        + [shape((2 * rows, WIDE), bf16)] * CHIPS,
        (me, decay_rates, skip_gain, decay_codes, b_proj, mixer_input, c_proj)
        + (gate_input, norm_gain.reshape(1, width), queries, keys),
        "shhhhhhhhhh",
        [
            pltpu.SMEM((heads,), f32),
            pltpu.SMEM((heads,), f32),
            pltpu.SemaphoreType.DMA((16,)),
        ],
    )
    other = swapped(state)
    qk_two = shifted(qk_two, 2)
    own, lead = call(
        within_kernel,
        [shape((rows, width), f32)] * 2,
        (slope, skips, codes, b, x, c, gate),
        "",
    )
    chip_state = call(chip_kernel, half_state, (me, slope, state, other), "s")
    chip_other = lax.ppermute(chip_state, "seq", [(i, i ^ 2) for i in range(n)])
    two_chips, qk_one = call(
        two_chips_kernel,
        [half_state, shape((2 * rows, WIDE), bf16)],
        (me, own, slope, chip_state, chip_other, qk_one),
        "savvva",
        through=1,
    )
    far = lax.ppermute(two_chips, "seq", [(i, i + 4) for i in range(n // 2)])
    ahead, qk_three = call(
        ahead_kernel,
        [shape((HD, width // 2), bf16), shape((2 * rows, WIDE), bf16)],
        (me, qk_two, slope, chip_other, far, qk_three),
        "savvva",
        through=1,
    )
    qk = [qk_own, shifted(qk_one, 1), qk_two, shifted(qk_three, 3)]
    gated, squares = call(
        gated_kernel,
        [shape((rows, width), f32), shape((8, rows), f32)],
        (me, slope, other, ahead, swapped(ahead), own, lead, c),
        "s",
    )
    squares = [squares] + [
        lax.ppermute(squares, "head", [(i, (i + k) % m) for i in range(m)]) for k in range(1, m)
    ]
    mamba_out, *values = call(
        functools.partial(norm_kernel, width * m),
        [jax.ShapeDtypeStruct((rows, width), bf16)] + [chunk] * CHIPS,
        (me, gain, gated, *squares),
        "s",
    )
    values = exchange(values)
    own_keys = call(
        keys_kernel,
        shape((CHIPS * rows, WIDE), bf16),
        (me, values[0], *qk),
        "sa",
    )
    weights = call(
        weights_kernel,
        shape((2, CHIPS * rows, n * rows), bf16),
        (me, own_keys, swapped(own_keys), *qk),
        "s",
        [pltpu.VMEM((CHIPS * rows, WIDE), bf16)],
        limit=24 * MIB,
    )
    passed = [call(passed_kernel, chunk, (weights, part), "a") for part in values[1:]]
    other_values = [swapped(part) for part in (values[0], *passed)]
    partial_sums = call(
        own_values_kernel,
        shape((CHIPS * rows, WIDE), f32),
        (me, weights, *values),
        "s",
        [pltpu.VMEM((CHIPS * rows, WIDE), bf16)],
    )
    results = call(
        values_kernel,
        [chunk] * CHIPS,
        (me, partial_sums, weights, *other_values),
        "s",
        [pltpu.VMEM((CHIPS * rows, WIDE), bf16), pltpu.VMEM((CHIPS * rows, WIDE), bf16)],
    )
    attn_out = call(
        join_kernel,
        jax.ShapeDtypeStruct((rows, width), bf16),
        (me, *exchange(results)),
        "s",
    )
    return (mamba_out, attn_out)


def running_sum(log_decay):
    span = log_decay.shape[1]
    at = jnp.arange(span, dtype=jnp.int32)
    earlier = (at[:, None] <= at[None, :]).astype(jnp.float32)
    return jnp.dot(log_decay, earlier, precision=HIGH)


def carried_in(array, axis, combine, identity):
    devices, mine = (lax.axis_size(axis), lax.axis_index(axis))
    everything = jax.tree.map(
        lambda part, kind: lax.all_gather(part.astype(kind), axis),
        array,
        (jnp.bfloat16, jnp.bfloat16),
    )
    start = jax.tree.map(
        lambda part, zero: jnp.broadcast_to(jnp.asarray(zero, part.dtype), part.shape),
        array,
        identity,
    )

    def hop(k, before):
        reached = k < mine
        new = combine(
            before, jax.tree.map(lambda part, own: part[k].astype(own.dtype), everything, array)
        )
        return jax.tree.map(lambda a, b: jnp.where(reached, a, b), new, before)

    return lax.fori_loop(0, devices, hop, start)


def block_step(state_carry, inputs):
    x_block, b_block, c_block, decay_block = inputs
    running = running_sum(decay_block)
    span = decay_block.shape[1]
    causal = (
        jnp.arange(span, dtype=jnp.int32)[:, None] >= jnp.arange(span, dtype=jnp.int32)[None, :]
    )
    log_gaps = jnp.where(causal[None, :, :], running[:, :, None] - running[:, None, :], NEG)
    decays = jnp.exp(log_gaps)
    match_strength = jnp.dot(c_block, b_block.T, preferred_element_type=jnp.float32)
    x_float = x_block.astype(jnp.float32)
    within = jnp.einsum(
        "hts,shp->thp", decays * match_strength[None, :, :], x_float, precision=HIGH
    )
    c_float = c_block.astype(jnp.float32)
    carried = jnp.exp(running).T[:, :, None] * jnp.einsum(
        "tn,hnp->thp", c_float, state_carry, precision=HIGH
    )
    to_end = jnp.exp(running[:, -1:] - running)
    updated_state = jnp.exp(running[:, -1])[:, None, None] * state_carry + jnp.einsum(
        "hs,sn,shp->hnp", to_end, b_block.astype(jnp.float32), x_float, precision=HIGH
    )
    return (updated_state, within + carried)


def local_scan(x_local, b_local, c_local, log_decay):
    tok_rows = x_local.shape[0]
    heads_local = log_decay.shape[0]
    block_count = tok_rows // BLOCK
    x_blocks = x_local.reshape(block_count, BLOCK, heads_local, CHANNELS_PER_HD)
    b_blocks = b_local.reshape(block_count, BLOCK, b_local.shape[1])
    c_blocks = c_local.reshape(block_count, BLOCK, c_local.shape[1])
    decay_blocks = log_decay.reshape(heads_local, block_count, BLOCK).transpose(1, 0, 2)
    initial = jnp.zeros((heads_local, b_local.shape[1], CHANNELS_PER_HD), jnp.float32)
    final_state, y_blocks = lax.scan(
        block_step, initial, (x_blocks, b_blocks, c_blocks, decay_blocks)
    )
    return (final_state, y_blocks.reshape(tok_rows, heads_local, CHANNELS_PER_HD))


def masked_scores(q_rows, q_pos, k_rows, k_pos):
    score_scale = 1.0 / math.sqrt(k_rows.shape[-1])
    scores = (
        jnp.einsum("qhd,khd->hqk", q_rows, k_rows, preferred_element_type=jnp.float32) * score_scale
    )
    visible = k_pos[None, None, :] <= q_pos[None, :, None]
    return (jnp.where(visible, scores, NEG), visible)


def online_update(group_state, q_rows, q_pos, k_rows, v_rows, k_pos):
    row_top, row_total, weighted_sum = group_state
    scores, visible = masked_scores(q_rows, q_pos, k_rows, k_pos)
    new_top = jnp.maximum(row_top, jnp.max(scores, axis=2))
    rescale = jnp.exp(row_top - new_top)
    weights = jnp.where(visible, jnp.exp(scores - new_top[:, :, None]), 0.0)
    row_total = row_total * rescale + jnp.sum(weights, axis=2)
    weighted_sum = weighted_sum * rescale[:, :, None] + jnp.einsum(
        "hqk,khd->hqd", weights.astype(jnp.bfloat16), v_rows, preferred_element_type=jnp.float32
    )
    return (new_top, row_total, weighted_sum)


def when_visible(state_update, group_state, q_pos, key_offset):
    return lax.cond(key_offset > q_pos[-1], lambda held: held, state_update, group_state)


def gathered(
    mixer_input,
    gate_input,
    b_proj,
    c_proj,
    decay_codes,
    decay_rates,
    skip_gain,
    norm_gain,
    queries,
    keys,
):
    tok_rows = mixer_input.shape[0]
    heads_local = decay_rates.shape[0]
    heads_att = queries.shape[1] // HD
    seq_rank = lax.axis_index("seq")
    own_positions = seq_rank * tok_rows + jnp.arange(tok_rows, dtype=jnp.int32)
    groups = [(queries, own_positions)]
    groups = [(q_rows.reshape(q_rows.shape[0], heads_att, HD), q_pos) for q_rows, q_pos in groups]
    log_decay = -decay_rates[:, None] * decay_codes.astype(jnp.float32)
    local_state, y_local = local_scan(mixer_input, b_proj, c_proj, log_decay)
    total_log = jnp.sum(log_decay, axis=1)

    def combine(earlier, later):
        return (earlier[0] + later[0], jnp.exp(later[0])[:, None, None] * earlier[1] + later[1])

    identity = (jnp.zeros_like(total_log), jnp.zeros_like(local_state))
    _, incoming = carried_in((total_log, local_state), "seq", combine, identity)
    running = running_sum(log_decay)
    carried = jnp.einsum("tn,hnp->thp", c_proj.astype(jnp.float32), incoming, precision=HIGH)
    carried = carried * jnp.exp(running).T[:, :, None]
    x_float = mixer_input.reshape(tok_rows, heads_local, CHANNELS_PER_HD).astype(jnp.float32)
    ssm_out = (y_local + carried + skip_gain[None, :, None] * x_float).reshape(
        tok_rows, heads_local * CHANNELS_PER_HD
    )
    gated = ssm_out * jax.nn.silu(gate_input.astype(jnp.float32))
    squares = lax.psum(jnp.sum(gated * gated, axis=1), "head")
    channels = gated.shape[1] * lax.axis_size("head")
    mamba_out = (
        gated * lax.rsqrt(squares / channels + 1e-05)[:, None] * norm_gain[None, :]
    ).astype(jnp.bfloat16)
    initial = tuple(
        (
            (
                jnp.full((heads_att, q_pos.shape[0]), NEG, jnp.float32),
                jnp.zeros((heads_att, q_pos.shape[0]), jnp.float32),
                jnp.zeros((heads_att, q_pos.shape[0], HD), jnp.float32),
            )
            for _, q_pos in groups
        )
    )
    states = initial
    k_piece = lax.all_gather(keys, "seq", axis=0, tiled=True)
    v_piece = lax.all_gather(mamba_out, "seq", axis=0, tiled=True)
    row_count = k_piece.shape[0]
    block_rows = math.gcd(row_count, 512)

    def one_block(block_id, states):
        key_offset = block_id * block_rows
        k_rows = lax.dynamic_slice_in_dim(k_piece, block_id * block_rows, block_rows, 0).reshape(
            block_rows, heads_att, HD
        )
        v_rows = lax.dynamic_slice_in_dim(v_piece, block_id * block_rows, block_rows, 0).reshape(
            block_rows, heads_att, HD
        )
        k_pos = key_offset + jnp.arange(block_rows, dtype=jnp.int32)
        return tuple(
            (
                when_visible(
                    functools.partial(
                        online_update,
                        q_rows=group[0],
                        q_pos=group[1],
                        k_rows=k_rows,
                        v_rows=v_rows,
                        k_pos=k_pos,
                    ),
                    group_state,
                    group[1],
                    key_offset,
                )
                for group, group_state in zip(groups, states)
            )
        )

    finals = lax.fori_loop(0, row_count // block_rows, one_block, states)
    results = [(group_state[2], group_state[1]) for group_state in finals]
    rows_out = [
        (weighted / totals[:, :, None])
        .transpose(1, 0, 2)
        .reshape(weighted.shape[1], heads_att * HD)
        .astype(jnp.bfloat16)
        for weighted, totals in results
    ]
    attn_out = rows_out[0]
    return (mamba_out, attn_out)


def on_device(mixer_input, gate_input, b_proj, c_proj, decay_codes, *others):
    n = lax.axis_size("seq")
    rows, width = mixer_input.shape
    fits = (
        n == 2 * CHIPS
        and width == n * HD
        and decay_codes.shape[0] == 2 * n
        and b_proj.shape[1] == HD
        and rows == BLOCK
    )
    return (two_heads_each if fits else gathered)(
        mixer_input, gate_input, b_proj, c_proj, decay_codes, *others
    )


def solution(mesh):
    in_specs = (
        P("seq", "head"),
        P("seq", "head"),
        P("seq", None),
        P("seq", None),
        P("head", "seq"),
        P("head"),
        P("head"),
        P("head"),
        P("seq", "head"),
        P("seq", "head"),
    )
    out_specs = (P("seq", "head"), P("seq", "head"))
    return jax.shard_map(
        on_device, mesh=mesh, in_specs=in_specs, out_specs=out_specs, check_vma=False
    )
```

```python
import functools
import math

import jax
import jax.numpy as jnp
from jax import lax
from jax.experimental import pallas as pl
from jax.experimental.pallas import tpu as pltpu
from jax.sharding import PartitionSpec as P

HD = 128
CHANNELS_PER_HD = 64
BLOCK = 256


HIGH = lax.Precision.HIGHEST
NEG = -1e30
LOG2E = 1.4426950408889634
MIB = 1 << 20


VMEM = pl.BlockSpec(memory_space=pltpu.VMEM)
SMEM = pl.BlockSpec(memory_space=pltpu.SMEM)
HBM = pl.BlockSpec(memory_space=pltpu.HBM)
ANY = pl.BlockSpec(memory_space=pl.ANY)
CHIPS = 4
WIDE = 2 * HD
PARTS = 16


def call(body, outs, args, spaces, scratch=(), limit=16 * MIB, through=0):
    kinds = {"s": SMEM, "h": HBM, "a": ANY, "v": VMEM}
    spaces = spaces + "v" * (len(args) - len(spaces))
    return pl.pallas_call(
        body,
        out_shape=outs,
        in_specs=[kinds[space] for space in spaces],
        out_specs=[ANY if i >= len(outs) - through else VMEM for i in range(len(outs))]
        if through
        else jax.tree.map(lambda _: VMEM, outs),
        input_output_aliases={len(args) - i: len(outs) - i for i in range(1, through + 1)},
        scratch_shapes=list(scratch),
        compiler_params=pltpu.CompilerParams(vmem_limit_bytes=limit),
        cost_estimate=pl.CostEstimate(flops=0, bytes_accessed=0, transcendentals=0),
    )(
        *(
            pltpu.with_memory_space_constraint(arg, pltpu.HBM) if space == "h" else arg
            for arg, space in zip(args, spaces)
        )
    )


def nt(a, b):
    return lax.dot_general(a, b, (((1,), (1,)), ((), ())), preferred_element_type=jnp.float32)


def nn(a, b):
    return jnp.dot(a, b, preferred_element_type=jnp.float32)


def step_counts(codes):
    rows = codes.shape[1]
    r = lax.broadcasted_iota(jnp.int32, (rows, rows), 0)
    s = lax.broadcasted_iota(jnp.int32, (rows, rows), 1)
    upper = (r <= s).astype(jnp.float32).astype(jnp.bfloat16)
    lower = (s <= r).astype(jnp.float32).astype(jnp.bfloat16)
    high = lax.shift_right_logical(codes, 7).astype(jnp.float32).astype(jnp.bfloat16)
    low = (codes & 127).astype(jnp.float32).astype(jnp.bfloat16)
    return (
        128.0 * nn(high, upper) + nn(low, upper),
        128.0 * nt(lower, high) + nt(lower, low),
    )


def left_lanes(rows):
    return lax.broadcasted_iota(jnp.int32, (rows, HD), 1) < CHANNELS_PER_HD


def chip_of(me):
    return lax.shift_right_logical(me, 1)


def across(chip, by):
    return chip ^ by


def block_of(index, size):
    return pl.ds(pl.multiple_of(index * size, size), size)


def as_parts(total):
    total = jnp.broadcast_to(total, (PARTS, total.shape[1])).astype(jnp.int32)
    part = lax.broadcasted_iota(jnp.int32, total.shape, 0)
    high = lax.shift_right_logical(total, 16)
    middle = lax.shift_right_logical(total, 8) & 255
    chosen = jnp.where(
        part == 0, high, jnp.where(part == 1, middle, jnp.where(part == 2, total & 255, 0))
    )
    return chosen.astype(jnp.float32).astype(jnp.bfloat16)


def opened(rows):
    rows = rows.astype(jnp.float32)
    total = 65536.0 * rows[HD : HD + 1] + 256.0 * rows[HD + 1 : HD + 2] + rows[HD + 2 : HD + 3]
    return rows[:HD], total


def followed(first, second, slope):
    return jnp.exp2(second[1] * slope) * first[0] + second[0], first[1] + second[1]


def chunk_pairs(chip, steps, q_hbm, k_hbm, outs):
    rows = q_hbm.shape[0]
    pairs = []
    for d, out in zip(steps, outs):
        cols = block_of(across(chip, d), WIDE)
        pairs.append((q_hbm.at[:, cols], out.at[pl.ds(0, rows), :]))
        pairs.append((k_hbm.at[:, cols], out.at[pl.ds(rows, rows), :]))
    return pairs


def first_kernel(
    me_ref, rates_hbm, skip_hbm, codes_hbm, b_hbm, x_hbm, c_hbm, gate_hbm, gain_hbm, q_hbm, k_hbm,
    state_ref, slope_ref, skips_ref, codes_ref, b_ref, x_ref, c_ref, gate_ref, gain_ref, *rest
):
    qk, (rates_ref, skip_ref, sems) = rest[:CHIPS], rest[CHIPS:]
    rows = x_ref.shape[0]
    chip = chip_of(me_ref[0])
    pairs = [
        (codes_hbm, codes_ref),
        (b_hbm, b_ref),
        (rates_hbm, rates_ref),
        (x_hbm, x_ref),
        (skip_hbm, skip_ref),
        (c_hbm, c_ref),
        (gate_hbm, gate_ref),
        (gain_hbm, gain_ref),
    ]
    pairs += chunk_pairs(chip, (0, 1, 2, 3), q_hbm, k_hbm, qk)
    copies = [pltpu.make_async_copy(a, b, sems.at[i]) for i, (a, b) in enumerate(pairs)]
    for copy in copies:
        copy.start()
    copies[0].wait()
    _, counts = step_counts(codes_ref[...])
    copies[1].wait()
    b_turned = b_ref[...].astype(jnp.float32).T.astype(jnp.bfloat16)
    left = left_lanes(rows)
    copies[2].wait()
    copies[3].wait()
    for pair in range(x_ref.shape[1] // HD):
        cols = slice(pair * HD, (pair + 1) * HD)
        one, two = rates_ref[2 * pair], rates_ref[2 * pair + 1]
        slope_ref[:, cols] = jnp.where(left_lanes(8), one, two) * -LOG2E
        column = jnp.where(left, counts[:, 2 * pair : 2 * pair + 1], counts[:, 2 * pair + 1 : 2 * pair + 2])
        total = column[rows - 1 : rows, :]
        weight = jnp.exp2((total - column) * slope_ref[0:1, cols])
        x = (x_ref[:, cols].astype(jnp.float32) * weight).astype(jnp.bfloat16)
        state_ref[pl.ds(0, HD), cols] = nn(b_turned, x).astype(jnp.bfloat16)
        state_ref[pl.ds(HD, PARTS), cols] = as_parts(total)
    copies[4].wait()
    for pair in range(x_ref.shape[1] // HD):
        cols = slice(pair * HD, (pair + 1) * HD)
        skips_ref[:, cols] = jnp.where(left_lanes(8), skip_ref[2 * pair], skip_ref[2 * pair + 1])
    for copy in copies[5:]:
        copy.wait()


def chip_kernel(me_ref, slope_ref, own_ref, other_ref, out_ref):
    core = me_ref[0] & 1
    half = own_ref.shape[1] // 2
    cols = block_of(core, half)
    own, other = own_ref[:, cols], other_ref[:, cols]
    first = opened(jnp.where(core == 0, own, other))
    second = opened(jnp.where(core == 0, other, own))
    state, total = followed(first, second, slope_ref[0:1, cols])
    out_ref[pl.ds(0, HD), :] = state.astype(jnp.bfloat16)
    out_ref[pl.ds(HD, PARTS), :] = as_parts(total)


def two_chips_kernel(me_ref, after_ref, slope_ref, own_ref, other_ref, *rest):
    out_ref = rest[1]
    me = me_ref[0]
    odd = chip_of(me) & 1
    own, other = own_ref[...], other_ref[...]
    first = opened(jnp.where(odd == 0, own, other))
    second = opened(jnp.where(odd == 0, other, own))
    state, total = followed(first, second, slope_ref[0:1, block_of(me & 1, own.shape[1])])
    out_ref[pl.ds(0, HD), :] = state.astype(jnp.bfloat16)
    out_ref[pl.ds(HD, PARTS), :] = as_parts(total)


def ahead_kernel(me_ref, after_ref, slope_ref, other_ref, far_ref, *rest):
    me = me_ref[0]
    odd = chip_of(me) & 1
    near, total = opened(other_ref[...])
    near = jnp.where(odd == 1, near, 0.0)
    total = jnp.where(odd == 1, total, 0.0)
    far, _ = opened(far_ref[...])
    slope = slope_ref[0:1, block_of(me & 1, near.shape[1])]
    rest[1][...] = (jnp.exp2(total * slope) * far + near).astype(jnp.bfloat16)


def within_kernel(slope_ref, skips_ref, codes_ref, b_ref, x_ref, c_ref, gate_ref, own_ref, lead_ref):
    rows = x_ref.shape[0]
    across, down = step_counts(codes_ref[...])
    t = lax.broadcasted_iota(jnp.int32, (rows, rows), 0)
    s = lax.broadcasted_iota(jnp.int32, (rows, rows), 1)
    match = jnp.where(s <= t, nt(c_ref[...], b_ref[...]), 0.0)
    left = left_lanes(rows)
    for pair in range(x_ref.shape[1] // HD):
        cols = slice(pair * HD, (pair + 1) * HD)
        x = x_ref[:, cols]
        ys = []
        leads = []
        for h in (2 * pair, 2 * pair + 1):
            slope = slope_ref[0:1, h * CHANNELS_PER_HD : h * CHANNELS_PER_HD + 1]
            gap = jnp.maximum(down[:, h : h + 1] - across[h : h + 1, :], 0.0)
            ys.append(nn((jnp.exp2(gap * slope) * match).astype(jnp.bfloat16), x))
            leads.append(jnp.exp2(down[:, h : h + 1] * slope))
        gate = gate_ref[:, cols].astype(jnp.float32)
        gate = gate / (1.0 + jnp.exp(-gate))
        given = jnp.where(left, ys[0], ys[1]) + skips_ref[0:1, cols] * x.astype(jnp.float32)
        own_ref[:, cols] = given * gate
        lead_ref[:, cols] = jnp.where(left, leads[0], leads[1]) * gate


def gated_kernel(
    me_ref, slope_ref, local_ref, ahead_ref, other_ref, own_ref, lead_ref, c_ref, gated_ref, squares_ref
):
    core = me_ref[0] & 1
    c = c_ref[...]
    ones = jnp.ones((8, HD), jnp.bfloat16)
    squares = jnp.zeros(squares_ref.shape, jnp.float32)
    half = ahead_ref.shape[1]
    for at in range(0, 2 * half, HD):
        cols, within = slice(at, at + HD), slice(at % half, at % half + HD)
        state = jnp.where(core == at // half, ahead_ref[:, within], other_ref[:, within])
        state = state.astype(jnp.float32)
        later, _ = followed((state, 0.0), opened(local_ref[:, cols]), slope_ref[0:1, cols])
        state = jnp.where(core == 1, later, state).astype(jnp.bfloat16)
        gated = own_ref[:, cols] + lead_ref[:, cols] * nn(c, state)
        gated_ref[:, cols] = gated
        square = gated * gated
        high = square.astype(jnp.bfloat16)
        low = (square - high.astype(jnp.float32)).astype(jnp.bfloat16)
        squares = squares + nt(ones, high) + nt(ones, low)
    squares_ref[...] = squares


def turned(row):
    size = row.shape[1]
    r = lax.broadcasted_iota(jnp.int32, (size, size), 0)
    s = lax.broadcasted_iota(jnp.int32, (size, size), 1)
    return jnp.sum(jnp.where(r == s, jnp.broadcast_to(row, (size, size)), 0.0), axis=1, keepdims=True)


def norm_kernel(channels, me_ref, gain_ref, gated_ref, *rest):
    squares, out_ref, parts = rest[: -1 - CHIPS], rest[-1 - CHIPS], rest[-CHIPS:]
    chip = chip_of(me_ref[0])
    total = squares[0][0:1, :]
    for part in squares[1:]:
        total = total + part[0:1, :]
    column = turned(lax.rsqrt(total / channels + 1e-05))
    for d in range(CHIPS):
        cols = block_of(across(chip, d), WIDE)
        out = (gated_ref[:, cols] * column * gain_ref[:, cols]).astype(jnp.bfloat16)
        parts[d][...] = out
        out_ref[:, cols] = out


def keys_kernel(me_ref, after_ref, *rest):
    chip = chip_of(me_ref[0])
    rows = rest[0].shape[0] // 2
    for d in range(CHIPS):
        rest[CHIPS][block_of(across(chip, d), rows), :] = rest[d][pl.ds(rows, rows), :]


def weights_kernel(me_ref, own_ref, other_ref, *rest):
    ins, out_ref, q_ref = rest[:CHIPS], rest[CHIPS], rest[CHIPS + 1]
    rows = ins[0].shape[0] // 2
    me = me_ref[0]
    chip, core = chip_of(me), me & 1
    for d in range(CHIPS):
        q_ref[block_of(across(chip, d), rows), :] = ins[d][pl.ds(0, rows), :]
    scale = LOG2E / math.sqrt(HD)
    half = rows // 2
    for head in range(2):
        lanes = slice(head * HD, (head + 1) * HD)
        for i in range(2 * CHIPS):
            seen = (i // 2) * rows
            q = q_ref[pl.ds(i * half, half), lanes]
            t = lax.broadcasted_iota(jnp.int32, (half, rows), 0) + (i % 2) * half
            s = lax.broadcasted_iota(jnp.int32, (half, rows), 1)
            blocks = []
            for keys_ref, base, shown in (
                (own_ref, 0, s <= t),
                (other_ref, CHIPS * rows, s < core * rows),
            ):
                for at in range(0, seen, rows):
                    blocks.append((base + at, nt(q, keys_ref[pl.ds(at, rows), lanes])))
                last = nt(q, keys_ref[pl.ds(seen, rows), lanes])
                blocks.append((base + seen, jnp.where(shown, last, NEG)))
            top = functools.reduce(jnp.maximum, [block for _, block in blocks])
            top = jnp.max(top, axis=1, keepdims=True) * scale
            blocks = [(at, jnp.exp2(block * scale - top)) for at, block in blocks]
            total = functools.reduce(jnp.add, [block for _, block in blocks])
            inverse = 1.0 / jnp.sum(total, axis=1, keepdims=True)
            for at, block in blocks:
                out_ref[head, pl.ds(i * half, half), pl.ds(at, rows)] = (block * inverse).astype(
                    jnp.bfloat16
                )


def passed_kernel(after_ref, in_ref, out_ref):
    out_ref[...] = in_ref[...]


def weighted(weights_ref, head, i, rows, base, v_ref):
    seen = (i + 1) * rows
    lanes = slice(head * HD, (head + 1) * HD)
    held = weights_ref[head, pl.ds(i * rows, rows), pl.ds(base, seen)]
    return nn(held, v_ref[pl.ds(0, seen), lanes])


def in_place(me_ref, parts, v_ref):
    chip = chip_of(me_ref[0])
    for d, part in enumerate(parts):
        v_ref[block_of(across(chip, d), part.shape[0]), :] = part[...]


def own_values_kernel(me_ref, weights_ref, *rest):
    own, out_ref, v_ref = rest[:CHIPS], rest[CHIPS], rest[CHIPS + 1]
    rows = own[0].shape[0]
    in_place(me_ref, own, v_ref)
    for i in range(CHIPS):
        for head in range(2):
            lanes = slice(head * HD, (head + 1) * HD)
            out_ref[pl.ds(i * rows, rows), lanes] = weighted(weights_ref, head, i, rows, 0, v_ref)


def values_kernel(me_ref, partial_ref, weights_ref, *rest):
    other, outs, v_ref, o_ref = rest[:CHIPS], rest[CHIPS : 2 * CHIPS], *rest[2 * CHIPS :]
    rows = other[0].shape[0]
    in_place(me_ref, other, v_ref)
    for i in range(CHIPS):
        for head in range(2):
            at, lanes = pl.ds(i * rows, rows), slice(head * HD, (head + 1) * HD)
            more = weighted(weights_ref, head, i, rows, CHIPS * rows, v_ref)
            o_ref[at, lanes] = (partial_ref[at, lanes] + more).astype(jnp.bfloat16)
    chip = chip_of(me_ref[0])
    for d in range(CHIPS):
        outs[d][...] = o_ref[block_of(across(chip, d), rows), :]


def join_kernel(steps, me_ref, *rest):
    chip = chip_of(me_ref[0])
    for d, part in zip(steps, rest[:CHIPS]):
        rest[CHIPS][:, block_of(across(chip, d), WIDE)] = part[...]


def shifted(part, d):
    return lax.ppermute(part, "seq", [(i, i ^ (2 * d)) for i in range(2 * CHIPS)])


def exchange(parts):
    moved = {d: shifted(parts[d], d) for d in (3, 1, 2)}
    return [parts[0]] + [moved[d] for d in range(1, CHIPS)]


def swapped(part):
    return lax.ppermute(part, "seq", [(i, i ^ 1) for i in range(2 * CHIPS)])


def two_heads_each(
    mixer_input,
    gate_input,
    b_proj,
    c_proj,
    decay_codes,
    decay_rates,
    skip_gain,
    norm_gain,
    queries,
    keys,
):
    n, m = lax.axis_size("seq"), lax.axis_size("head")
    rows, width = mixer_input.shape
    heads = decay_codes.shape[0]
    me = lax.axis_index("seq").astype(jnp.int32).reshape(1)
    shape = pltpu.VMEM
    bf16, f32 = jnp.bfloat16, jnp.float32
    chunk = shape((rows, WIDE), bf16)
    half_state = shape((HD + PARTS, width // 2), bf16)

    state, slope, skips, codes, b, x, c, gate, gain, qk_own, qk_one, qk_two, qk_three = call(
        first_kernel,
        [shape((HD + PARTS, width), bf16), shape((8, width), f32), shape((8, width), f32)]
        + [
            shape(decay_codes.shape, jnp.int32),
            shape(b_proj.shape, bf16),
            shape((rows, width), bf16),
            shape(c_proj.shape, bf16),
            shape((rows, width), bf16),
            shape((1, width), f32),
        ]
        + [shape((2 * rows, WIDE), bf16)] * CHIPS,
        (me, decay_rates, skip_gain, decay_codes, b_proj, mixer_input, c_proj)
        + (gate_input, norm_gain.reshape(1, width), queries, keys),
        "shhhhhhhhhh",
        [
            pltpu.SMEM((heads,), f32),
            pltpu.SMEM((heads,), f32),
            pltpu.SemaphoreType.DMA((16,)),
        ],
    )
    other = swapped(state)
    qk_two = shifted(qk_two, 2)
    own, lead = call(
        within_kernel,
        [shape((rows, width), f32)] * 2,
        (slope, skips, codes, b, x, c, gate),
        "",
    )
    chip_state = call(chip_kernel, half_state, (me, slope, state, other), "s")
    chip_other = lax.ppermute(chip_state, "seq", [(i, i ^ 2) for i in range(n)])
    two_chips, qk_one = call(
        two_chips_kernel,
        [half_state, shape((2 * rows, WIDE), bf16)],
        (me, own, slope, chip_state, chip_other, qk_one),
        "savvva",
        through=1,
    )
    far = lax.ppermute(two_chips, "seq", [(i, i + 4) for i in range(n // 2)])
    ahead, qk_three = call(
        ahead_kernel,
        [shape((HD, width // 2), bf16), shape((2 * rows, WIDE), bf16)],
        (me, qk_two, slope, chip_other, far, qk_three),
        "savvva",
        through=1,
    )
    qk = [qk_own, shifted(qk_one, 1), qk_two, shifted(qk_three, 3)]
    gated, squares = call(
        gated_kernel,
        [shape((rows, width), f32), shape((8, rows), f32)],
        (me, slope, other, ahead, swapped(ahead), own, lead, c),
        "s",
    )
    squares = [squares] + [
        lax.ppermute(squares, "head", [(i, (i + k) % m) for i in range(m)]) for k in range(1, m)
    ]
    mamba_out, *values = call(
        functools.partial(norm_kernel, width * m),
        [jax.ShapeDtypeStruct((rows, width), bf16)] + [chunk] * CHIPS,
        (me, gain, gated, *squares),
        "s",
    )
    values = exchange(values)
    own_keys = call(
        keys_kernel,
        shape((CHIPS * rows, WIDE), bf16),
        (me, values[0], *qk),
        "sa",
    )
    weights = call(
        weights_kernel,
        shape((2, CHIPS * rows, n * rows), bf16),
        (me, own_keys, swapped(own_keys), *qk),
        "s",
        [pltpu.VMEM((CHIPS * rows, WIDE), bf16)],
        limit=24 * MIB,
    )
    passed = [call(passed_kernel, chunk, (weights, part), "a") for part in values[1:]]
    other_values = [swapped(part) for part in (values[0], *passed)]
    partial_sums = call(
        own_values_kernel,
        shape((CHIPS * rows, WIDE), f32),
        (me, weights, *values),
        "s",
        [pltpu.VMEM((CHIPS * rows, WIDE), bf16)],
    )
    results = call(
        values_kernel,
        [chunk] * CHIPS,
        (me, partial_sums, weights, *other_values),
        "s",
        [pltpu.VMEM((CHIPS * rows, WIDE), bf16), pltpu.VMEM((CHIPS * rows, WIDE), bf16)],
    )
    steps = (0, 3, 1, 2)
    results = exchange(results)
    attn_out = call(
        functools.partial(join_kernel, steps),
        jax.ShapeDtypeStruct((rows, width), bf16),
        (me, *(results[d] for d in steps)),
        "s",
    )
    return (mamba_out, attn_out)


def running_sum(log_decay):
    span = log_decay.shape[1]
    at = jnp.arange(span, dtype=jnp.int32)
    earlier = (at[:, None] <= at[None, :]).astype(jnp.float32)
    return jnp.dot(log_decay, earlier, precision=HIGH)


def carried_in(array, axis, combine, identity):
    devices, mine = (lax.axis_size(axis), lax.axis_index(axis))
    everything = jax.tree.map(
        lambda part, kind: lax.all_gather(part.astype(kind), axis),
        array,
        (jnp.bfloat16, jnp.bfloat16),
    )
    start = jax.tree.map(
        lambda part, zero: jnp.broadcast_to(jnp.asarray(zero, part.dtype), part.shape),
        array,
        identity,
    )

    def hop(k, before):
        reached = k < mine
        new = combine(
            before, jax.tree.map(lambda part, own: part[k].astype(own.dtype), everything, array)
        )
        return jax.tree.map(lambda a, b: jnp.where(reached, a, b), new, before)

    return lax.fori_loop(0, devices, hop, start)


def block_step(state_carry, inputs):
    x_block, b_block, c_block, decay_block = inputs
    running = running_sum(decay_block)
    span = decay_block.shape[1]
    causal = (
        jnp.arange(span, dtype=jnp.int32)[:, None] >= jnp.arange(span, dtype=jnp.int32)[None, :]
    )
    log_gaps = jnp.where(causal[None, :, :], running[:, :, None] - running[:, None, :], NEG)
    decays = jnp.exp(log_gaps)
    match_strength = jnp.dot(c_block, b_block.T, preferred_element_type=jnp.float32)
    x_float = x_block.astype(jnp.float32)
    within = jnp.einsum(
        "hts,shp->thp", decays * match_strength[None, :, :], x_float, precision=HIGH
    )
    c_float = c_block.astype(jnp.float32)
    carried = jnp.exp(running).T[:, :, None] * jnp.einsum(
        "tn,hnp->thp", c_float, state_carry, precision=HIGH
    )
    to_end = jnp.exp(running[:, -1:] - running)
    updated_state = jnp.exp(running[:, -1])[:, None, None] * state_carry + jnp.einsum(
        "hs,sn,shp->hnp", to_end, b_block.astype(jnp.float32), x_float, precision=HIGH
    )
    return (updated_state, within + carried)


def local_scan(x_local, b_local, c_local, log_decay):
    tok_rows = x_local.shape[0]
    heads_local = log_decay.shape[0]
    block_count = tok_rows // BLOCK
    x_blocks = x_local.reshape(block_count, BLOCK, heads_local, CHANNELS_PER_HD)
    b_blocks = b_local.reshape(block_count, BLOCK, b_local.shape[1])
    c_blocks = c_local.reshape(block_count, BLOCK, c_local.shape[1])
    decay_blocks = log_decay.reshape(heads_local, block_count, BLOCK).transpose(1, 0, 2)
    initial = jnp.zeros((heads_local, b_local.shape[1], CHANNELS_PER_HD), jnp.float32)
    final_state, y_blocks = lax.scan(
        block_step, initial, (x_blocks, b_blocks, c_blocks, decay_blocks)
    )
    return (final_state, y_blocks.reshape(tok_rows, heads_local, CHANNELS_PER_HD))


def masked_scores(q_rows, q_pos, k_rows, k_pos):
    score_scale = 1.0 / math.sqrt(k_rows.shape[-1])
    scores = (
        jnp.einsum("qhd,khd->hqk", q_rows, k_rows, preferred_element_type=jnp.float32) * score_scale
    )
    visible = k_pos[None, None, :] <= q_pos[None, :, None]
    return (jnp.where(visible, scores, NEG), visible)


def online_update(group_state, q_rows, q_pos, k_rows, v_rows, k_pos):
    row_top, row_total, weighted_sum = group_state
    scores, visible = masked_scores(q_rows, q_pos, k_rows, k_pos)
    new_top = jnp.maximum(row_top, jnp.max(scores, axis=2))
    rescale = jnp.exp(row_top - new_top)
    weights = jnp.where(visible, jnp.exp(scores - new_top[:, :, None]), 0.0)
    row_total = row_total * rescale + jnp.sum(weights, axis=2)
    weighted_sum = weighted_sum * rescale[:, :, None] + jnp.einsum(
        "hqk,khd->hqd", weights.astype(jnp.bfloat16), v_rows, preferred_element_type=jnp.float32
    )
    return (new_top, row_total, weighted_sum)


def when_visible(state_update, group_state, q_pos, key_offset):
    return lax.cond(key_offset > q_pos[-1], lambda held: held, state_update, group_state)


def gathered(
    mixer_input,
    gate_input,
    b_proj,
    c_proj,
    decay_codes,
    decay_rates,
    skip_gain,
    norm_gain,
    queries,
    keys,
):
    tok_rows = mixer_input.shape[0]
    heads_local = decay_rates.shape[0]
    heads_att = queries.shape[1] // HD
    seq_rank = lax.axis_index("seq")
    own_positions = seq_rank * tok_rows + jnp.arange(tok_rows, dtype=jnp.int32)
    groups = [(queries, own_positions)]
    groups = [(q_rows.reshape(q_rows.shape[0], heads_att, HD), q_pos) for q_rows, q_pos in groups]
    log_decay = -decay_rates[:, None] * decay_codes.astype(jnp.float32)
    local_state, y_local = local_scan(mixer_input, b_proj, c_proj, log_decay)
    total_log = jnp.sum(log_decay, axis=1)

    def combine(earlier, later):
        return (earlier[0] + later[0], jnp.exp(later[0])[:, None, None] * earlier[1] + later[1])

    identity = (jnp.zeros_like(total_log), jnp.zeros_like(local_state))
    _, incoming = carried_in((total_log, local_state), "seq", combine, identity)
    running = running_sum(log_decay)
    carried = jnp.einsum("tn,hnp->thp", c_proj.astype(jnp.float32), incoming, precision=HIGH)
    carried = carried * jnp.exp(running).T[:, :, None]
    x_float = mixer_input.reshape(tok_rows, heads_local, CHANNELS_PER_HD).astype(jnp.float32)
    ssm_out = (y_local + carried + skip_gain[None, :, None] * x_float).reshape(
        tok_rows, heads_local * CHANNELS_PER_HD
    )
    gated = ssm_out * jax.nn.silu(gate_input.astype(jnp.float32))
    squares = lax.psum(jnp.sum(gated * gated, axis=1), "head")
    channels = gated.shape[1] * lax.axis_size("head")
    mamba_out = (
        gated * lax.rsqrt(squares / channels + 1e-05)[:, None] * norm_gain[None, :]
    ).astype(jnp.bfloat16)
    initial = tuple(
        (
            (
                jnp.full((heads_att, q_pos.shape[0]), NEG, jnp.float32),
                jnp.zeros((heads_att, q_pos.shape[0]), jnp.float32),
                jnp.zeros((heads_att, q_pos.shape[0], HD), jnp.float32),
            )
            for _, q_pos in groups
        )
    )
    states = initial
    k_piece = lax.all_gather(keys, "seq", axis=0, tiled=True)
    v_piece = lax.all_gather(mamba_out, "seq", axis=0, tiled=True)
    row_count = k_piece.shape[0]
    block_rows = math.gcd(row_count, 512)

    def one_block(block_id, states):
        key_offset = block_id * block_rows
        k_rows = lax.dynamic_slice_in_dim(k_piece, block_id * block_rows, block_rows, 0).reshape(
            block_rows, heads_att, HD
        )
        v_rows = lax.dynamic_slice_in_dim(v_piece, block_id * block_rows, block_rows, 0).reshape(
            block_rows, heads_att, HD
        )
        k_pos = key_offset + jnp.arange(block_rows, dtype=jnp.int32)
        return tuple(
            (
                when_visible(
                    functools.partial(
                        online_update,
                        q_rows=group[0],
                        q_pos=group[1],
                        k_rows=k_rows,
                        v_rows=v_rows,
                        k_pos=k_pos,
                    ),
                    group_state,
                    group[1],
                    key_offset,
                )
                for group, group_state in zip(groups, states)
            )
        )

    finals = lax.fori_loop(0, row_count // block_rows, one_block, states)
    results = [(group_state[2], group_state[1]) for group_state in finals]
    rows_out = [
        (weighted / totals[:, :, None])
        .transpose(1, 0, 2)
        .reshape(weighted.shape[1], heads_att * HD)
        .astype(jnp.bfloat16)
        for weighted, totals in results
    ]
    attn_out = rows_out[0]
    return (mamba_out, attn_out)


def on_device(mixer_input, gate_input, b_proj, c_proj, decay_codes, *others):
    n = lax.axis_size("seq")
    rows, width = mixer_input.shape
    fits = (
        n == 2 * CHIPS
        and width == n * HD
        and decay_codes.shape[0] == 2 * n
        and b_proj.shape[1] == HD
        and rows == BLOCK
    )
    return (two_heads_each if fits else gathered)(
        mixer_input, gate_input, b_proj, c_proj, decay_codes, *others
    )


def solution(mesh):
    in_specs = (
        P("seq", "head"),
        P("seq", "head"),
        P("seq", None),
        P("seq", None),
        P("head", "seq"),
        P("head"),
        P("head"),
        P("head"),
        P("seq", "head"),
        P("seq", "head"),
    )
    out_specs = (P("seq", "head"), P("seq", "head"))
    return jax.shard_map(
        on_device, mesh=mesh, in_specs=in_specs, out_specs=out_specs, check_vma=False
    )
```
